256 devices in a mesh: seq: 64 (over y, z, core), mp: 4 (over x).
Axes of the slice: x: 4, y: 4, z: 8, core: 2. Of those that a mesh axis runs over, the one named last changes fastest.
Arguments:
- query: bfloat16 [16384, 2048], P('seq', 'mp'), may hold values from -5 to 5
- key: bfloat16 [16384, 2048], P('seq', 'mp'), may hold values from -5 to 5
- value: bfloat16 [16384, 2048], P('seq', 'mp'), may hold values from -6 to 6
- feat_query: bfloat16 [16384, 256], P('seq', 'mp'), may hold values from -4 to 4
- feat_key: bfloat16 [16384, 256], P('seq', 'mp'), may hold values from -4 to 4
- log_decay: float32 [16, 16384], P('mp', 'seq'), may hold values from -0.5 to 0
- band_width: int32 [256], P('seq'), may hold values from 16 to 64, as said below
- norm_gain: float32 [2048], P('mp'), may hold values from 0.5 to 1.5
- out_weight: bfloat16 [2048, 2048], P('mp'), may hold values from -0.125 to 0.125
- grad_out: bfloat16 [16384, 2048], P(('seq', 'mp')), may hold values from -6 to 6
Outputs:
- layer_out: bfloat16 [16384, 2048], P(('seq', 'mp'))
- grad_query: bfloat16 [16384, 2048], P('seq', 'mp')
- grad_key: bfloat16 [16384, 2048], P('seq', 'mp')
- grad_value: bfloat16 [16384, 2048], P('seq', 'mp')
- grad_feat_query: bfloat16 [16384, 256], P('seq', 'mp')
- grad_feat_key: bfloat16 [16384, 256], P('seq', 'mp')
The draws below stay inside these ranges and needn't reach their ends.
Inputs may be any that keep to these rules, and one draw needn't show every extreme that they name: `band_width`: entry b is the window width of query rows b * 64 to (b + 1) * 64 - 1; the first block of some device other than the first has width 64.
All inputs are finite; a program needn't handle non-finite values.
Results may differ from the reference program's by a relative error of at most 0.015.
Values may be sent and summed in bfloat16 or wider, within the bound.
No kernel may reach another device: no remote copies, remote signals or barrier semaphores. Data moves between devices by JAX's collectives and lax.ppermute only.
A program may use at most 128 MiB of HBM per device.

```python
import math
import jax
import jax.numpy as jnp
from jax import lax

D = 2048
HEAD_TOTAL = 16
HSIZE = 128
FEAT = 16
WINDOW = 64
BLOCK = 128
TOK_DEV = 256
TOKEN_TOTAL = 16384
HD = 2048
FD = 256
FSTATE = 273
N_SEQ = 64


def drawn_pair(key):
    base = jax.random.fold_in(key, 11)
    divided_keys = jax.random.split(base, 2)
    queries = jnp.clip(jax.random.normal(divided_keys[0], (TOKEN_TOTAL, HD), jnp.float32), -4.5, 4.5)
    keys_drawn = jnp.clip(jax.random.normal(divided_keys[1], (TOKEN_TOTAL, HD), jnp.float32), -4.5, 4.5)
    return (queries, keys_drawn)


def draw_query(key, part):
    return drawn_pair(key)[0].astype(jnp.bfloat16)


def draw_key(key, part):
    return drawn_pair(key)[1].astype(jnp.bfloat16)


def draw_log_decay(key, part):
    base = jax.random.fold_in(key, 23)
    divided_keys = jax.random.split(base, 5)
    pick = jax.random.uniform(divided_keys[0], (HEAD_TOTAL, 1), jnp.float32)
    slowness = jnp.minimum(1.0, 2.0 * pick)
    fast = math.log(1.0 / 40.0)
    slow = math.log(0.5 * math.log(10.0) / TOKEN_TOTAL)
    decay_rate = jnp.exp(fast + (slow - fast) * slowness)
    shards = TOKEN_TOTAL // TOK_DEV
    per_device_factor = jnp.exp(jax.random.uniform(divided_keys[1], (HEAD_TOTAL, shards, 1), jnp.float32, -math.log(2.0), math.log(2.0)))
    per_device_factor = jnp.broadcast_to(per_device_factor, (HEAD_TOTAL, shards, TOK_DEV)).reshape(HEAD_TOTAL, TOKEN_TOTAL)
    coarse_estimate = jax.random.uniform(divided_keys[2], (HEAD_TOTAL, TOKEN_TOTAL), jnp.float32, 0.5, 1.5)
    sudden_spike = jax.random.randint(divided_keys[3], (HEAD_TOTAL, TOKEN_TOTAL), 0, max(2, TOKEN_TOTAL // 2)) == 0
    dropped_fraction = jax.random.uniform(divided_keys[4], (HEAD_TOTAL, TOKEN_TOTAL), jnp.float32, math.log(1.25), math.log(1.5))
    return -(decay_rate * per_device_factor * coarse_estimate) - jnp.where(sudden_spike, dropped_fraction, 0.0)


def draw_band_width(key, part):
    count = TOKEN_TOTAL // WINDOW
    widths = jax.random.randint(jax.random.fold_in(key, 31), (count,), WINDOW // 4, WINDOW + 1)
    per_device = TOK_DEV // WINDOW
    chosen = jax.random.randint(jax.random.fold_in(key, 37), (), 1, TOKEN_TOTAL // TOK_DEV) * per_device
    return jnp.where(jnp.arange(count) == chosen, WINDOW, widths).astype(jnp.int32)


def shard_levels(key, dims, cuts, smallest, top_value):
    def one(axis_at, shards_of):
        heights = jax.random.uniform(jax.random.fold_in(jax.random.fold_in(key, 6), axis_at), (shards_of,), jnp.float32, smallest / len(cuts), top_value / len(cuts))
        return jnp.repeat(jnp.exp(heights), dims[axis_at] // shards_of).reshape((-1,) + (1,) * (len(dims) - axis_at - 1))

    level = one(*cuts[0])
    for cut in cuts[1:]:
        level = level * one(*cut)
    return level


def centred(key, dims, scale, bound, cuts=(), kind=jnp.bfloat16):
    values = jax.random.normal(key, dims, jnp.float32) * scale
    if len(cuts) > 0:
        values = shard_levels(key, dims, cuts, -0.22, 0.18) * values
    return jnp.clip(values, min=-bound, max=bound).astype(kind)


def setup_inputs(seed: int = 0) -> dict:
    streams_of = jax.random.split(jax.random.key(seed), 11)
    return {
        "query": draw_query(jax.random.fold_in(streams_of[10], 71), 0),
        "key": draw_key(jax.random.fold_in(streams_of[10], 71), 0),
        "value": centred(streams_of[2], (TOKEN_TOTAL, HD), 1.0, 6.0, ((0, 64), (1, 4))),
        "feat_query": centred(streams_of[3], (TOKEN_TOTAL, FD), 1.0, 4.0, ((0, 64), (1, 4))),
        "feat_key": centred(streams_of[4], (TOKEN_TOTAL, FD), 1.0, 4.0, ((0, 64), (1, 4))),
        "log_decay": draw_log_decay(jax.random.fold_in(streams_of[10], 71), 0),
        "band_width": draw_band_width(jax.random.fold_in(streams_of[10], 71), 0),
        "norm_gain": jnp.clip(1.0 + 0.1 * jax.random.normal(streams_of[7], (HD,), jnp.float32), 0.5, 1.5),
        "out_weight": centred(streams_of[8], (HD, D), HD ** -0.5, 0.125, ((0, 4),)),
        "grad_out": centred(streams_of[9], (TOKEN_TOTAL, D), 1.0, 6.0, ((0, 256),)),
    }


EPS = 1e-06
NEG = -1e+30
HIGH = lax.Precision.HIGHEST

def feature_map(values):
    width = values.shape[-1]
    ones = jnp.ones(values.shape[:-1] + (1,), jnp.float32)
    square = (values[..., :, None] * values[..., None, :]).reshape(values.shape[:-1] + (width * width,))
    return jnp.concatenate([ones, values * width ** (-0.25), square * (2.0 * width) ** (-0.5)], axis=-1)

def block_step(carry, inputs):
    state, offset = carry
    query_feats, key_feats, values, decay = inputs
    width = query_feats.shape[-1]
    count = decay.shape[1]
    within = jnp.cumsum(decay, axis=1)
    value_f = values.astype(jnp.float32)
    inner = jnp.einsum('thf,shf->hts', query_feats, key_feats, precision=HIGH) * width ** (-0.5)
    span = within[:, :, None] - within[:, None, :]
    causal = jnp.arange(count)[:, None] >= jnp.arange(count)[None, :]
    weights = jnp.where(causal[None], (1.0 + inner + 0.5 * inner * inner) * jnp.exp(jnp.minimum(span, 0.0)), 0.0)
    local = jnp.einsum('hts,shd->thd', weights, value_f, precision=HIGH)
    query_map = feature_map(query_feats) * jnp.exp(within).T[:, :, None]
    carried = jnp.einsum('thf,hfd->thd', query_map, state, precision=HIGH)
    key_map = feature_map(key_feats) * jnp.exp(within[:, -1:] - within).T[:, :, None]
    new_state = jnp.exp(within[:, -1])[:, None, None] * state + jnp.einsum('thf,thd->hfd', key_map, value_f, precision=HIGH)
    return ((new_state, offset + within[:, -1]), (local + carried, offset[:, None] + within))

def linear_scan(query_feats, key_feats, values, decay, block, state, offset):
    count, heads = (query_feats.shape[0], query_feats.shape[1])
    blocks = count // block

    def split(array):
        return array.reshape((blocks, block) + array.shape[1:])
    decay_blocks = decay.reshape(heads, blocks, block).transpose(1, 0, 2)
    (state, offset), (outputs, running) = lax.scan(jax.checkpoint(block_step), (state, offset), (split(query_feats), split(key_feats), split(values), decay_blocks))
    return (outputs.reshape(values.shape), state, running.transpose(1, 0, 2).reshape(heads, count))

def combine_heads(attended, linear, gain):
    scale = lax.rsqrt(lax.optimization_barrier(jnp.mean(linear * linear, axis=-1, keepdims=True)) + EPS)
    mixed = attended + linear * scale * gain.reshape(linear.shape[1], linear.shape[2])
    return mixed.reshape(linear.shape[0], linear.shape[1] * linear.shape[2])

def window_attend(query_in, keys_ext, values_ext, band, first, heads, window):
    count, width = query_in.shape
    size = width // heads
    blocks = count // window
    query_blocks = query_in.reshape(blocks, window, heads, size).astype(jnp.float32)
    key_blocks = keys_ext.reshape(blocks + 1, window, heads, size)
    value_blocks = values_ext.reshape(blocks + 1, window, heads, size)
    key_pair = jnp.concatenate([key_blocks[:-1], key_blocks[1:]], axis=1).astype(jnp.float32)
    value_pair = jnp.concatenate([value_blocks[:-1], value_blocks[1:]], axis=1).astype(jnp.float32)
    scores = jnp.einsum('bqhd,bkhd->bhqk', query_blocks, key_pair) * size ** (-0.5)
    back = window + jnp.arange(window)[:, None] - jnp.arange(2 * window)[None, :]
    key_place = first + jnp.arange(blocks)[:, None] * window - window + jnp.arange(2 * window)[None, :]
    allowed = (back[None] >= 0) & (back[None] < band[:, None, None]) & (key_place[:, None, :] >= 0)
    scores = jnp.where(allowed[:, None], scores, NEG)
    top = lax.stop_gradient(lax.optimization_barrier(jnp.max(scores, axis=-1, keepdims=True)))
    expo = jnp.exp(scores - top)
    weights = lax.optimization_barrier((expo / lax.optimization_barrier(jnp.sum(expo, axis=-1, keepdims=True))).astype(jnp.bfloat16))
    mixed = jnp.einsum('bhqk,bkhd->bqhd', weights.astype(jnp.float32), value_pair)
    return mixed.reshape(count, heads, size)

def reference(query, key, value, feat_query, feat_key, log_decay, band_width, norm_gain, out_weight, grad_out):
    bands = band_width.reshape(N_SEQ, TOK_DEV // WINDOW)
    firsts = jnp.arange(N_SEQ, dtype=jnp.int32) * TOK_DEV
    decay_groups = log_decay.reshape(HEAD_TOTAL, N_SEQ, TOK_DEV).transpose(1, 0, 2)

    def with_previous(array):
        grouped = array.reshape(N_SEQ, TOK_DEV, HD)
        previous = jnp.concatenate([jnp.zeros((1, WINDOW, HD), array.dtype), grouped[:-1, TOK_DEV - WINDOW:]], axis=0)
        return jnp.concatenate([previous, grouped], axis=1)

    def window_group(inputs):
        query_in, keys_in, values_in, band, first = inputs
        return window_attend(query_in, keys_in, values_in, band, first, HEAD_TOTAL, WINDOW)

    def group_step(carry, inputs):
        state, offset = carry
        query_feats, key_feats, values, decay = inputs
        outputs, state, running = linear_scan(query_feats, key_feats, values, decay, BLOCK, state, offset)
        return ((state, running[:, -1]), outputs)

    def forward(query_in, key_in, value_in, fquery_in, fkey_in):
        grouped_query = query_in.reshape(N_SEQ, TOK_DEV, HD)
        attended = lax.map(jax.checkpoint(window_group), (grouped_query, with_previous(key_in), with_previous(value_in), bands, firsts))
        attended = attended.reshape(TOKEN_TOTAL, HEAD_TOTAL, HSIZE)
        start = (jnp.zeros((HEAD_TOTAL, FSTATE, HSIZE), jnp.float32), jnp.zeros((HEAD_TOTAL,), jnp.float32))
        inputs = (fquery_in.reshape(N_SEQ, TOK_DEV, HEAD_TOTAL, FEAT), fkey_in.reshape(N_SEQ, TOK_DEV, HEAD_TOTAL, FEAT), value_in.reshape(N_SEQ, TOK_DEV, HEAD_TOTAL, HSIZE), decay_groups)
        _, linear = lax.scan(jax.checkpoint(group_step), start, inputs)
        linear = linear.reshape(TOKEN_TOTAL, HEAD_TOTAL, HSIZE)
        return combine_heads(attended, linear, norm_gain)
    fquery32 = feat_query.astype(jnp.float32)
    fkey32 = feat_key.astype(jnp.float32)
    mixed, backward = jax.vjp(forward, query, key, value, fquery32, fkey32)
    layer_out = jnp.dot(mixed.astype(jnp.bfloat16), out_weight, preferred_element_type=jnp.float32).astype(jnp.bfloat16)
    grad_mixed = jnp.dot(grad_out, out_weight.T, preferred_element_type=jnp.float32)
    grad_q, grad_k, grad_v, grad_fq, grad_fk = backward(grad_mixed)
    return (layer_out, grad_q, grad_k, grad_v, grad_fq.astype(jnp.bfloat16), grad_fk.astype(jnp.bfloat16))
```

```python
import numpy as np
import ml_dtypes
import jax
import jax.numpy as jnp
from jax import lax
from jax.experimental import pallas as pl
from jax.experimental.pallas import tpu as pltpu
from jax.sharding import PartitionSpec as P

WINDOW = 64
EPS = 1e-06
NEG = -1e30
F32 = jnp.float32
BF16 = jnp.bfloat16
TOK = 256
HEADS = 4
SIZE = 128
FEAT = 16
ROWS = 256
SCALE = SIZE**-0.5

NN = (((1,), (0,)), ((), ()))
NT = (((1,), (1,)), ((), ()))
TN = (((0,), (0,)), ((), ()))


def mm(a, b, dims):
    return lax.dot_general(a, b, dims, preferred_element_type=F32)


def selectors(query_side):
    first = np.zeros((ROWS, FEAT), np.float32)
    second = np.zeros_like(first)
    weight = [1 / 32] + [1 / 16] * 7 + [1 / 32, 1 / 4]
    for a in range(FEAT):
        for r in range(10):
            first[a * 16 + r, a] = weight[r] if query_side else 1.0
            if r < 9:
                second[a * 16 + r, (a + r) % FEAT] = 1.0
    both = np.concatenate([first, second], axis=0).astype(ml_dtypes.bfloat16)
    return (both, np.ascontiguousarray(both.T))


SEL_K, SEL_K_T = selectors(False)
SEL_Q, SEL_Q_T = selectors(True)


def row_kind(shape, dim):
    return lax.broadcasted_iota(jnp.int32, shape, dim) % 16


def factors_rows(feats_t, sel, const):
    both = mm(sel, feats_t, NN)
    kind = row_kind((ROWS, 1), 0)
    left = both[:ROWS, :] + jnp.where(kind == 10, const, 0.0)
    right = both[ROWS:, :] + jnp.where((kind == 9) | (kind == 10), 1.0, 0.0)
    return (left, right)


def factors_cols(feats_t, sel_t, const):
    both = mm(feats_t, sel_t, TN)
    kind = row_kind((1, ROWS), 1)
    left = both[:, :ROWS] + jnp.where(kind == 10, const, 0.0)
    right = both[:, ROWS:] + jnp.where((kind == 9) | (kind == 10), 1.0, 0.0)
    return (left, right)


def feature_grad(grad_phi, left, right, sel_t):
    both = jnp.concatenate([grad_phi * right, grad_phi * left], axis=0)
    return mm(sel_t, both.astype(BF16), NN)


def split3(value):
    hi = value.astype(BF16)
    rest = value - hi.astype(F32)
    mid = rest.astype(BF16)
    low = (rest - mid.astype(F32)).astype(BF16)
    return (hi, mid, low)


def with_total(state, total):
    kind = row_kind((ROWS, 1), 0)
    hi, mid, low = split3(total)
    state = jnp.where(kind == 11, hi.astype(F32), state)
    state = jnp.where(kind == 12, mid.astype(F32), state)
    return jnp.where(kind == 13, low.astype(F32), state)


def local_state_kernel(
    feat_t, value, key_tail, decay, sel, state_out, cum_out, cum_row_out, edge_out
):
    edge_out[:WINDOW, :] = key_tail[...]
    edge_out[WINDOW:, :] = value[TOK - WINDOW :, :]
    tri = (
        lax.broadcasted_iota(jnp.int32, (TOK, TOK), 0)
        >= lax.broadcasted_iota(jnp.int32, (TOK, TOK), 1)
    ).astype(F32).astype(BF16)
    parts = split3(decay[...])
    cum_row_out[:, 0, :] = sum(mm(p, tri, NT) for p in parts)
    for h in range(HEADS):
        cum = sum(
            mm(tri, jnp.broadcast_to(p[h : h + 1, :], (SIZE, TOK)), NT) for p in parts
        )
        cum_out[:, h * SIZE : (h + 1) * SIZE] = cum
        total = cum[TOK - 1 : TOK, :]
        rows = slice(h * ROWS, (h + 1) * ROWS)
        left, right = factors_rows(feat_t[h * FEAT : (h + 1) * FEAT, :], sel[...], 1.0)
        phi = (left * right).astype(BF16)
        scaled = value[:, h * SIZE : (h + 1) * SIZE].astype(F32) * jnp.exp(total - cum)
        state = mm(phi, scaled.astype(BF16), NN)
        state_out[rows, :] = with_total(state, total).astype(BF16)


def chain_kernel(reverse, arrived, before_out):
    count = arrived.shape[0]
    carry = jnp.zeros((16, SIZE), F32)
    order = range(count)
    for j in reversed(order) if reverse else order:
        before_out[j] = carry.astype(BF16)
        piece = arrived[j].astype(F32)
        total = piece[11:12] + piece[12:13] + piece[13:14]
        carry = carry * jnp.exp(total) + piece


def intra_weights(fq_t, fk_t, cum, cum_row):
    inner = mm(fq_t, fk_t, TN) * FEAT**-0.5
    span = jnp.concatenate([cum, cum], axis=1) - cum_row
    causal = lax.broadcasted_iota(jnp.int32, (TOK, TOK), 0) >= lax.broadcasted_iota(
        jnp.int32, (TOK, TOK), 1
    )
    fade = jnp.where(causal, jnp.exp(jnp.minimum(span, 0.0)), 0.0)
    return (inner, fade, (1.0 + inner + 0.5 * inner * inner) * fade)


def block_pair(before, array, b):
    if b == 0:
        return jnp.concatenate([before, array[:WINDOW, :]], axis=0)
    return array[(b - 1) * WINDOW : (b + 1) * WINDOW, :]


def intra_kernel(fq_t, fk_t, value, cum, cum_row, sel, sel_t, local_out, phi_out, phit_out):
    _, _, weights = intra_weights(fq_t[...], fk_t[...], cum[...], cum_row[0])
    local_out[...] = mm(weights.astype(BF16), value[...], NN)
    left, right = factors_cols(fq_t[...], sel_t[...], 1 / 16)
    phi_out[...] = (left * right).astype(BF16)
    left, right = factors_rows(fq_t[...], sel[...], 1 / 16)
    phit_out[...] = (left * right).astype(BF16)


def window_kernel(band, query, key, value, before, attended_out, probs_out):
    row = lax.broadcasted_iota(jnp.int32, (WINDOW, 2 * WINDOW), 0)
    col = lax.broadcasted_iota(jnp.int32, (WINDOW, 2 * WINDOW), 1)
    back = WINDOW + row - col
    for b in range(TOK // WINDOW):
        here = slice(b * WINDOW, (b + 1) * WINDOW)
        allowed = (back >= 0) & (back < band[b])
        if b == 0:
            allowed = allowed & (col >= band[TOK // WINDOW])
        for h in range(query.shape[1] // SIZE):
            cols = slice(h * SIZE, (h + 1) * SIZE)
            keys = block_pair(before[:WINDOW, cols], key.at[:, cols], b)
            values = block_pair(before[WINDOW:, cols], value.at[:, cols], b)
            scores = mm(query[here, cols], keys, NT) * SCALE
            scores = jnp.where(allowed, scores, NEG)
            expo = jnp.exp(scores - jnp.max(scores, axis=-1, keepdims=True))
            probs = expo / jnp.sum(expo, axis=-1, keepdims=True)
            probs16 = probs.astype(BF16)
            probs_out[here, cols] = probs16
            attended_out[here, cols] = mm(probs16, values, NN)


def window_grad_kernel(
    query, key, value, before, probs, grad_rows, weight, grad_out, gq_out, gk_out, gv_out, edge_out
):
    grad = mm(grad_rows[...], weight[...], NT)
    grad_out[...] = grad
    grad16 = grad.astype(BF16)
    for h in range(query.shape[1] // SIZE):
        cols = slice(h * SIZE, (h + 1) * SIZE)
        key_parts = []
        value_parts = []
        for b in range(TOK // WINDOW):
            here = slice(b * WINDOW, (b + 1) * WINDOW)
            keys = block_pair(before[:WINDOW, cols], key.at[:, cols], b)
            values = block_pair(before[WINDOW:, cols], value.at[:, cols], b)
            probs16 = probs[here, cols]
            probs32 = probs16.astype(F32)
            grad_here = grad16[here, cols]
            grad_probs = mm(grad_here, values, NT).astype(BF16).astype(F32)
            along = jnp.sum(probs32 * grad_probs, axis=-1, keepdims=True)
            grad_scores = (probs32 * (grad_probs - along) * SCALE).astype(BF16)
            gq_out[here, cols] = mm(grad_scores, keys, NN).astype(BF16)
            key_parts.append(mm(grad_scores, query[here, cols], TN).astype(BF16))
            value_parts.append(mm(probs16, grad_here, TN).astype(BF16))
        for place, parts, out in ((0, key_parts, gk_out), (WINDOW, value_parts, gv_out)):
            edge_out[place : place + WINDOW, cols] = parts[0][:WINDOW, :]
            for b in range(TOK // WINDOW):
                own = parts[b][WINDOW:, :]
                if b + 1 < TOK // WINDOW:
                    own = own + parts[b + 1][:WINDOW, :]
                out[b * WINDOW : (b + 1) * WINDOW, cols] = own


def mix_kernel(
    state, phi, phit, local, attended, grad, cum, gain, mixed_out, grad_linear_out, grad_state_out
):
    cum = cum[...]
    fade = jnp.exp(cum)
    linear = local[...] + fade * mm(phi[...], state[...], NN)
    scale = lax.rsqrt(jnp.mean(linear * linear, axis=-1, keepdims=True) + EPS)
    mixed_out[...] = (attended[...] + linear * scale * gain[...]).astype(BF16)
    scaled = grad[...] * gain[...]
    along = jnp.mean(scaled * linear, axis=-1, keepdims=True)
    grad_linear = scale * scaled - linear * (scale * scale * scale * along)
    grad_linear_out[...] = grad_linear.astype(BF16)
    grad_state = mm(phit[...], (grad_linear * fade).astype(BF16), NN)
    grad_state_out[...] = with_total(grad_state, cum[TOK - 1 : TOK, :]).astype(BF16)


def intra_grad_kernel(
    fq_t, fk_t, value, cum, cum_row, sel, sel_t, state, grad_linear, gq_out, gk_out, gv_out
):
    fq_t, fk_t, grads = (fq_t[...], fk_t[...], grad_linear[...])
    inner, fade, weights = intra_weights(fq_t, fk_t, cum[...], cum_row[0])
    gv_out[...] = mm(weights.astype(BF16), grads, TN)
    grad_inner = mm(grads, value[...], NT) * fade * (1.0 + inner) * FEAT**-0.5
    grad_inner = grad_inner.astype(BF16)
    gk_out[...] = mm(fq_t, grad_inner, NN)
    faded = (grads.astype(F32) * jnp.exp(cum[...])).astype(BF16)
    grad_phi = mm(state[...], faded, NT)
    left, right = factors_rows(fq_t, sel[...], 1 / 16)
    gq = mm(fk_t, grad_inner, NT) + feature_grad(grad_phi, left, right, sel_t[...])
    gq_out[...] = gq.astype(BF16)


def finish_kernel(
    fk_t, value, cum, sel, sel_t, suffix, gv_local, gk_local, window_key, window_value, edge,
    gk_out, gv_out, gfk_out
):
    cum = cum[...]
    fade = jnp.exp(cum[TOK - 1 : TOK, :] - cum)
    left, right = factors_cols(fk_t[...], sel_t[...], 1.0)
    carried = mm((left * right).astype(BF16), suffix[...], NN) * fade
    gv = (gv_local[...] + carried).astype(BF16)
    last = TOK - WINDOW
    gv_out[:last, :] = window_value[:last, :] + gv[:last, :]
    gv_out[last:, :] = (window_value[last:, :] + edge[WINDOW:, :]) + gv[last:, :]
    gk_out[:last, :] = window_key[:last, :]
    gk_out[last:, :] = window_key[last:, :] + edge[:WINDOW, :]
    faded = (value[...].astype(F32) * fade).astype(BF16)
    grad_phi = mm(suffix[...], faded, NT)
    left, right = factors_rows(fk_t[...], sel[...], 1.0)
    gfk_out[...] = (gk_local[...] + feature_grad(grad_phi, left, right, sel_t[...])).astype(BF16)


def shape(dims, kind):
    return jax.ShapeDtypeStruct(dims, kind)


def whole(*dims):
    return pl.BlockSpec(dims, lambda h: (0,) * len(dims))


def cols(rows, heads=1):
    return pl.BlockSpec((rows, heads * SIZE), lambda h: (0, h))


COLS = cols(TOK)
PAIR = cols(TOK, 2)
STATE = pl.BlockSpec((ROWS, SIZE), lambda h: (h, 0))
PHI = pl.BlockSpec((TOK, ROWS), lambda h: (0, h))
PHIT = pl.BlockSpec((ROWS, TOK), lambda h: (h, 0))
FEATS = pl.BlockSpec((FEAT, TOK), lambda h: (h, 0))
CROW = pl.BlockSpec((1, 1, TOK), lambda h: (h, 0, 0))
SEL = whole(2 * ROWS, FEAT)
SEL_T = whole(FEAT, 2 * ROWS)


def params(mib):
    return pltpu.CompilerParams(vmem_limit_bytes=mib << 20)


def cost(flops, moved):
    return pl.CostEstimate(flops=flops, transcendentals=0, bytes_accessed=moved)


def swap(value):
    return lax.all_to_all(value, "seq", split_axis=0, concat_axis=0, tiled=True)


def chain(arrived, reverse):
    return pl.pallas_call(
        lambda a, o: chain_kernel(reverse, a, o),
        out_shape=shape(arrived.shape, BF16),
        name="chain_back" if reverse else "chain_fwd",
        compiler_params=params(4),
        cost_estimate=cost(1 << 20, 1 << 19),
    )(arrived)


def after(value, *others):
    return lax.optimization_barrier((value, *others))


def shifted(value, ways, k):
    return lax.ppermute(value, "mp", [(i, (i + k) % ways) for i in range(ways)])


def body(
    query, key, value, feat_query, feat_key, log_decay, band_width, norm_gain, out_weight, grad_out
):
    count, width = query.shape
    peers = lax.axis_size("seq")
    place = lax.axis_index("seq")
    ways = lax.axis_size("mp")
    lane = lax.axis_index("mp")
    sel_k, sel_kt, sel_q, sel_qt = (jnp.asarray(m) for m in (SEL_K, SEL_K_T, SEL_Q, SEL_Q_T))
    wide32 = shape((count, width), F32)
    wide16 = shape((count, width), BF16)
    edge16 = shape((2 * WINDOW, width), BF16)
    states = shape((HEADS * ROWS, SIZE), BF16)
    chunks = (peers, HEADS * ROWS // peers, SIZE)
    fq_t, fk_t = (feat_query.T, feat_key.T)
    model = grad_out.shape[1]

    state, cum, cum_row, edge = pl.pallas_call(
        local_state_kernel,
        grid=(1,),
        in_specs=[
            whole(HEADS * FEAT, TOK),
            whole(TOK, width),
            pl.BlockSpec((WINDOW, width), lambda h: (TOK // WINDOW - 1, 0)),
            whole(HEADS, TOK),
            SEL,
        ],
        out_specs=[
            whole(HEADS * ROWS, SIZE),
            whole(TOK, width),
            whole(HEADS, 1, TOK),
            whole(2 * WINDOW, width),
        ],
        out_shape=[states, wide32, shape((HEADS, 1, TOK), F32), edge16],
        compiler_params=params(12),
        name="local_state",
    )(fk_t, value, key, log_decay, sel_k)

    arrived = swap(state.reshape(chunks))

    before = lax.ppermute(edge, "seq", [(i, i + 1) for i in range(peers - 1)])
    grad_pieces = [grad_out] + [shifted(grad_out, ways, k) for k in range(1, ways)]

    local, phi, phit = pl.pallas_call(
        intra_kernel,
        grid=(HEADS,),
        in_specs=[FEATS, FEATS, COLS, COLS, CROW, SEL, SEL_T],
        out_specs=[COLS, PHI, PHIT],
        out_shape=[wide32, shape((TOK, HEADS * ROWS), BF16), shape((HEADS * ROWS, TOK), BF16)],
        compiler_params=params(8),
        name="intra",
    )(fq_t, fk_t, value, cum, cum_row, sel_q, sel_qt)

    first_col = jnp.where(place == 0, WINDOW, 0).astype(jnp.int32)
    band = jnp.concatenate([band_width, first_col[None]])
    attended, probs = pl.pallas_call(
        window_kernel,
        grid=(HEADS // 2,),
        in_specs=[
            pl.BlockSpec(memory_space=pltpu.SMEM),
            PAIR,
            PAIR,
            PAIR,
            cols(2 * WINDOW, 2),
        ],
        out_specs=[PAIR, PAIR],
        out_shape=[wide32, wide16],
        compiler_params=params(8),
        name="window",
    )(band, query, key, value, before)

    arrived, attended, probs, local, phi, phit = after(
        arrived, attended, probs, local, phi, phit
    )
    prefix = swap(chain(arrived, False))

    grad_rows = jnp.zeros((ways, count // ways, model), BF16)
    for k, piece in enumerate(grad_pieces):
        grad_rows = lax.dynamic_update_slice(grad_rows, piece[None], ((lane - k) % ways, 0, 0))
    grad_rows = grad_rows.reshape(count, model)

    grad, grad_query, win_key, win_value, edge_grad = pl.pallas_call(
        window_grad_kernel,
        grid=(HEADS // 2,),
        in_specs=[
            PAIR,
            PAIR,
            PAIR,
            cols(2 * WINDOW, 2),
            PAIR,
            whole(TOK, model),
            pl.BlockSpec((2 * SIZE, model), lambda h: (h, 0)),
        ],
        out_specs=[PAIR, PAIR, PAIR, PAIR, cols(2 * WINDOW, 2)],
        out_shape=[wide32, wide16, wide16, wide16, edge16],
        compiler_params=params(12),
        name="window_grad",
    )(query, key, value, before, probs, grad_rows, out_weight)

    prefix, grad, win_key, win_value, edge_grad = after(
        prefix, grad, win_key, win_value, edge_grad
    )
    prefix = prefix.reshape(HEADS * ROWS, SIZE)

    mixed, grad_linear, grad_state = pl.pallas_call(
        mix_kernel,
        grid=(HEADS,),
        in_specs=[
            STATE, PHI, PHIT, COLS, COLS, COLS, COLS,
            pl.BlockSpec((1, SIZE), lambda h: (0, h)),
        ],
        out_specs=[COLS, COLS, STATE],
        out_shape=[wide16, wide16, states],
        compiler_params=params(8),
        name="mix",
    )(prefix, phi, phit, local, attended, grad, cum, norm_gain.reshape(1, width))

    arrived = swap(grad_state.reshape(chunks))

    returned = lax.ppermute(edge_grad, "seq", [(i + 1, i) for i in range(peers - 1)])
    partial = jnp.dot(mixed, out_weight, preferred_element_type=F32).astype(BF16)
    partial = partial.reshape(ways, count // ways, model)

    def piece_for(k):
        return lax.dynamic_index_in_dim(partial, (lane + k) % ways, 0, keepdims=False)

    sums = [piece_for(0)] + [shifted(piece_for(k), ways, k) for k in range(1, ways)]

    arrived, *sums = after(arrived, *sums)
    suffix = swap(chain(arrived, True))

    gq_t, gk_local, gv_local = pl.pallas_call(
        intra_grad_kernel,
        grid=(HEADS,),
        in_specs=[FEATS, FEATS, COLS, COLS, CROW, SEL, SEL_T, STATE, COLS],
        out_specs=[FEATS, FEATS, COLS],
        out_shape=[
            shape((HEADS * FEAT, TOK), BF16),
            shape((HEADS * FEAT, TOK), F32),
            wide32,
        ],
        compiler_params=params(8),
        name="intra_grad",
    )(fq_t, fk_t, value, cum, cum_row, sel_q, sel_qt, prefix, grad_linear)
    layer_out = sum(p.astype(F32) for p in sums).astype(BF16)

    suffix, gk_local, gv_local, layer_out = after(suffix, gk_local, gv_local, layer_out)

    grad_key, grad_value, gfk_t = pl.pallas_call(
        finish_kernel,
        grid=(HEADS,),
        in_specs=[
            FEATS, COLS, COLS, SEL, SEL_T, STATE, COLS, FEATS, COLS, COLS, cols(2 * WINDOW),
        ],
        out_specs=[COLS, COLS, FEATS],
        out_shape=[wide16, wide16, shape((HEADS * FEAT, TOK), BF16)],
        compiler_params=params(8),
        name="finish",
    )(
        fk_t, value, cum, sel_k, sel_kt, suffix.reshape(HEADS * ROWS, SIZE), gv_local, gk_local,
        win_key, win_value, returned,
    )
    return (layer_out, grad_query, grad_key, grad_value, gq_t.T, gfk_t.T)


def solution(mesh):
    return jax.shard_map(
        body,
        mesh=mesh,
        in_specs=(
            P("seq", "mp"),
            P("seq", "mp"),
            P("seq", "mp"),
            P("seq", "mp"),
            P("seq", "mp"),
            P("mp", "seq"),
            P("seq"),
            P("mp"),
            P("mp", None),
            P(("seq", "mp"), None),
        ),
        out_specs=(
            P(("seq", "mp"), None),
            P("seq", "mp"),
            P("seq", "mp"),
            P("seq", "mp"),
            P("seq", "mp"),
            P("seq", "mp"),
        ),
        check_vma=False,
    )
```

```python
import numpy as np
import ml_dtypes
import jax
import jax.numpy as jnp
from jax import lax
from jax.experimental import pallas as pl
from jax.experimental.pallas import tpu as pltpu
from jax.sharding import PartitionSpec as P

WINDOW = 64
EPS = 1e-06
NEG = -1e30
F32 = jnp.float32
BF16 = jnp.bfloat16
TOK = 256
HEADS = 4
SIZE = 128
FEAT = 16
ROWS = 256
SCALE = SIZE**-0.5

NN = (((1,), (0,)), ((), ()))
NT = (((1,), (1,)), ((), ()))
TN = (((0,), (0,)), ((), ()))


def mm(a, b, dims):
    return lax.dot_general(a, b, dims, preferred_element_type=F32)


def selectors(query_side):
    first = np.zeros((ROWS, FEAT), np.float32)
    second = np.zeros_like(first)
    weight = [1 / 32] + [1 / 16] * 7 + [1 / 32, 1 / 4]
    for a in range(FEAT):
        for r in range(10):
            first[a * 16 + r, a] = weight[r] if query_side else 1.0
            if r < 9:
                second[a * 16 + r, (a + r) % FEAT] = 1.0
    both = np.concatenate([first, second], axis=0).astype(ml_dtypes.bfloat16)
    return (both, np.ascontiguousarray(both.T))


SEL_K, SEL_K_T = selectors(False)
SEL_Q, SEL_Q_T = selectors(True)


def row_kind(shape, dim):
    return lax.broadcasted_iota(jnp.int32, shape, dim) % 16


def factors_rows(feats_t, sel, const):
    both = mm(sel, feats_t, NN)
    kind = row_kind((ROWS, 1), 0)
    left = both[:ROWS, :] + jnp.where(kind == 10, const, 0.0)
    right = both[ROWS:, :] + jnp.where((kind == 9) | (kind == 10), 1.0, 0.0)
    return (left, right)


def factors_cols(feats_t, sel_t, const):
    both = mm(feats_t, sel_t, TN)
    kind = row_kind((1, ROWS), 1)
    left = both[:, :ROWS] + jnp.where(kind == 10, const, 0.0)
    right = both[:, ROWS:] + jnp.where((kind == 9) | (kind == 10), 1.0, 0.0)
    return (left, right)


def feature_grad(grad_phi, left, right, sel_t):
    both = jnp.concatenate([grad_phi * right, grad_phi * left], axis=0)
    return mm(sel_t, both.astype(BF16), NN)


def split3(value):
    hi = value.astype(BF16)
    rest = value - hi.astype(F32)
    mid = rest.astype(BF16)
    low = (rest - mid.astype(F32)).astype(BF16)
    return (hi, mid, low)


def with_total(state, total):
    kind = row_kind((ROWS, 1), 0)
    hi, mid, low = split3(total)
    state = jnp.where(kind == 11, hi.astype(F32), state)
    state = jnp.where(kind == 12, mid.astype(F32), state)
    return jnp.where(kind == 13, low.astype(F32), state)


def head_cols(h):
    return slice(h * SIZE, (h + 1) * SIZE)


def head_rows(h):
    return slice(h * ROWS, (h + 1) * ROWS)


def head_feats(h):
    return slice(h * FEAT, (h + 1) * FEAT)


def local_state_kernel(
    feat_t, decay, sel, value_far, key_far, query_far,
    state_out, cum_out, cum_row_out, edge_out, faded_out, value, key, query, sems
):
    first = pltpu.make_async_copy(value_far, value, sems.at[0])
    first.start()
    others = [
        pltpu.make_async_copy(far, near, sems.at[1 + i])
        for i, (far, near) in enumerate(((key_far, key), (query_far, query)))
    ]
    for copy in others:
        copy.start()
    tri = (
        lax.broadcasted_iota(jnp.int32, (TOK, TOK), 0)
        >= lax.broadcasted_iota(jnp.int32, (TOK, TOK), 1)
    ).astype(F32).astype(BF16)
    parts = split3(decay[...])
    cum_row_out[:, 0, :] = sum(mm(p, tri, NT) for p in parts)
    cum_all = sum(mm(tri, p, NT) for p in parts)
    cum_out[...] = cum_all
    first.wait()
    for h in range(HEADS):
        cum = cum_all[:, h : h + 1]
        total = cum[TOK - 1 : TOK, :]
        left, right = factors_rows(feat_t[head_feats(h), :], sel[...], 1.0)
        phi = (left * right).astype(BF16)
        faded = (value[:, head_cols(h)].astype(F32) * jnp.exp(total - cum)).astype(BF16)
        faded_out[:, head_cols(h)] = faded
        state = mm(phi, faded, NN)
        state_out[head_rows(h), :] = with_total(state, total).astype(BF16)
    for copy in others:
        copy.wait()
    edge_out[:WINDOW, :] = key[TOK - WINDOW :, :]
    edge_out[WINDOW:, :] = value[TOK - WINDOW :, :]


def chain_kernel(reverse, arrived, before_out):
    count = arrived.shape[0]
    carry = jnp.zeros((16, SIZE), F32)
    order = range(count)
    for j in reversed(order) if reverse else order:
        before_out[j] = carry.astype(BF16)
        piece = arrived[j].astype(F32)
        total = piece[11:12] + piece[12:13] + piece[13:14]
        carry = carry * jnp.exp(total) + piece


def intra_weights(fq_t, fk_t, cum, cum_row):
    inner = mm(fq_t, fk_t, TN) * FEAT**-0.5
    span = cum - cum_row
    causal = lax.broadcasted_iota(jnp.int32, (TOK, TOK), 0) >= lax.broadcasted_iota(
        jnp.int32, (TOK, TOK), 1
    )
    fade = jnp.where(causal, jnp.exp(jnp.minimum(span, 0.0)), 0.0)
    return (inner, fade, (1.0 + inner + 0.5 * inner * inner) * fade)


def block_pair(before, array, b):
    if b == 0:
        return jnp.concatenate([before, array[:WINDOW, :]], axis=0)
    return array[(b - 1) * WINDOW : (b + 1) * WINDOW, :]


def intra_kernel(fq_t, fk_t, value, cum, cum_row, sel, sel_t, local_out, phi_out, phit_out):
    for h in range(HEADS):
        feats = fq_t[head_feats(h), :]
        _, _, weights = intra_weights(
            feats, fk_t[head_feats(h), :], cum[:, h : h + 1], cum_row[h]
        )
        local_out[:, head_cols(h)] = mm(weights.astype(BF16), value[:, head_cols(h)], NN)
        left, right = factors_cols(feats, sel_t[...], 1 / 16)
        phi_out[:, head_rows(h)] = (left * right).astype(BF16)
        left, right = factors_rows(feats, sel[...], 1 / 16)
        phit_out[head_rows(h), :] = (left * right).astype(BF16)


def window_kernel(band, first_col, query, key, value, before, attended_out, probs_out):
    row = lax.broadcasted_iota(jnp.int32, (WINDOW, 2 * WINDOW), 0)
    col = lax.broadcasted_iota(jnp.int32, (WINDOW, 2 * WINDOW), 1)
    back = WINDOW + row - col
    for b in range(TOK // WINDOW):
        here = slice(b * WINDOW, (b + 1) * WINDOW)
        allowed = (back >= 0) & (back < band[b])
        if b == 0:
            allowed = allowed & (col >= first_col[0])
        for h in range(HEADS):
            cols = head_cols(h)
            keys = block_pair(before[:WINDOW, cols], key.at[:, cols], b)
            values = block_pair(before[WINDOW:, cols], value.at[:, cols], b)
            scores = mm(query[here, cols], keys, NT) * SCALE
            scores = jnp.where(allowed, scores, NEG)
            expo = jnp.exp(scores - jnp.max(scores, axis=-1, keepdims=True))
            probs = expo / jnp.sum(expo, axis=-1, keepdims=True)
            probs16 = probs.astype(BF16)
            probs_out[here, cols] = probs16
            attended_out[here, cols] = mm(probs16, values, NN).astype(BF16)


def window_grad_kernel(
    place, query, key, value, before, probs, piece0, piece1, piece2, piece3, weight_far,
    grad_out, gq_out, gk_out, gv_out, edge_out, rows, weight, sems
):
    pieces = (piece0, piece1, piece2, piece3)
    half = weight.shape[0] // 2
    copies = []
    for k, piece in enumerate(pieces):
        at = ((place[0] + (len(pieces) - k)) % len(pieces)) * WINDOW
        to = rows.at[pl.ds(pl.multiple_of(at, WINDOW), WINDOW), :]
        copies.append(pltpu.make_async_copy(piece, to, sems.at[k]))
    for i in range(2):
        part = slice(i * half, (i + 1) * half)
        copies.append(
            pltpu.make_async_copy(weight_far.at[part, :], weight.at[part, :], sems.at[4 + i])
        )
    for copy in copies:
        copy.start()
    for copy in copies[:5]:
        copy.wait()
    for h in range(HEADS):
        cols = head_cols(h)
        if h % 2 == 0:
            if h > 0:
                copies[5].wait()
            pair = slice(h * SIZE, (h + 2) * SIZE)
            grad16 = mm(rows[...], weight[pair, :], NT).astype(BF16)
            grad_out[:, pair] = grad16
        mine = head_cols(h % 2)
        key_parts = []
        value_parts = []
        for b in range(TOK // WINDOW):
            here = slice(b * WINDOW, (b + 1) * WINDOW)
            keys = block_pair(before[:WINDOW, cols], key.at[:, cols], b)
            values = block_pair(before[WINDOW:, cols], value.at[:, cols], b)
            probs16 = probs[here, cols]
            probs32 = probs16.astype(F32)
            grad_here = grad16[here, mine]
            grad_probs = mm(grad_here, values, NT).astype(BF16).astype(F32)
            along = jnp.sum(probs32 * grad_probs, axis=-1, keepdims=True)
            grad_scores = (probs32 * (grad_probs - along) * SCALE).astype(BF16)
            gq_out[here, cols] = mm(grad_scores, keys, NN).astype(BF16)
            key_parts.append(mm(grad_scores, query[here, cols], TN).astype(BF16))
            value_parts.append(mm(probs16, grad_here, TN).astype(BF16))
        for at, parts, out in ((0, key_parts, gk_out), (WINDOW, value_parts, gv_out)):
            edge_out[at : at + WINDOW, cols] = parts[0][:WINDOW, :]
            for b in range(TOK // WINDOW):
                own = parts[b][WINDOW:, :]
                if b + 1 < TOK // WINDOW:
                    own = own + parts[b + 1][:WINDOW, :]
                out[b * WINDOW : (b + 1) * WINDOW, cols] = own


def mix_kernel(
    state, phi, phit, local, attended, grad, cum, gain, grad_state_out, mixed_out, grad_linear_out
):
    for h in range(HEADS):
        cols = head_cols(h)
        steps = cum[:, h : h + 1]
        fade = jnp.exp(steps)
        linear = local[:, cols] + fade * mm(phi[:, head_rows(h)], state[head_rows(h), :], NN)
        scale = lax.rsqrt(jnp.mean(linear * linear, axis=-1, keepdims=True) + EPS)
        gains = gain[:, cols]
        mixed_out[:, cols] = (attended[:, cols].astype(F32) + linear * scale * gains).astype(BF16)
        scaled = grad[:, cols].astype(F32) * gains
        along = jnp.mean(scaled * linear, axis=-1, keepdims=True)
        grad_linear = scale * scaled - linear * (scale * scale * scale * along)
        grad_linear_out[:, cols] = grad_linear.astype(BF16)
        grad_state = mm(phit[head_rows(h), :], (grad_linear * fade).astype(BF16), NN)
        total = steps[TOK - 1 : TOK, :]
        grad_state_out[head_rows(h), :] = with_total(grad_state, total).astype(BF16)


def project_kernel(place, mixed, weight_far, piece0, piece1, piece2, piece3, rows, weight, sems):
    pieces = (piece0, piece1, piece2, piece3)
    step = weight.shape[1] // len(pieces)
    parts = [slice(i * step, (i + 1) * step) for i in range(len(pieces))]
    copies = [
        pltpu.make_async_copy(weight_far.at[:, part], weight.at[:, part], sems.at[i])
        for i, part in enumerate(parts)
    ]
    for copy in copies:
        copy.start()
    for k in range(len(pieces)):
        at = ((place[0] + k) % len(pieces)) * WINDOW
        rows[k * WINDOW : (k + 1) * WINDOW, :] = mixed[pl.ds(pl.multiple_of(at, WINDOW), WINDOW), :]
    for copy, part in zip(copies, parts):
        copy.wait()
        product = mm(rows[...], weight[:, part], NN).astype(BF16)
        for k, piece in enumerate(pieces):
            piece[:, part] = product[k * WINDOW : (k + 1) * WINDOW, :]


def intra_grad_kernel(
    fq_t, fk_t, value, cum, cum_row, sel, sel_t, state, grad_linear, gq_out, gk_out, gv_out
):
    for h in range(HEADS):
        cols = head_cols(h)
        fq, fk, grads = (fq_t[head_feats(h), :], fk_t[head_feats(h), :], grad_linear[:, cols])
        steps = cum[:, h : h + 1]
        inner, fade, weights = intra_weights(fq, fk, steps, cum_row[h])
        gv_out[:, cols] = mm(weights.astype(BF16), grads, TN)
        grad_inner = mm(grads, value[:, cols], NT) * fade * (1.0 + inner) * FEAT**-0.5
        grad_inner = grad_inner.astype(BF16)
        gk_out[head_feats(h), :] = mm(fq, grad_inner, NN)
        faded = (grads.astype(F32) * jnp.exp(steps)).astype(BF16)
        grad_phi = mm(state[head_rows(h), :], faded, NT)
        left, right = factors_rows(fq, sel[...], 1 / 16)
        gq = mm(fk, grad_inner, NT) + feature_grad(grad_phi, left, right, sel_t[...])
        gq_out[head_feats(h), :] = gq.astype(BF16)


def finish_kernel(
    fk_t, faded, cum, sel, sel_t, suffix, gv_local, gk_local, window_key, window_value, edge,
    gk_out, gv_out, gfk_out
):
    last = TOK - WINDOW
    gk_out[:last, :] = window_key[:last, :]
    gk_out[last:, :] = window_key[last:, :] + edge[:WINDOW, :]
    for h in range(HEADS):
        cols = head_cols(h)
        fk = fk_t[head_feats(h), :]
        steps = cum[:, h : h + 1]
        fade = jnp.exp(steps[TOK - 1 : TOK, :] - steps)
        left, right = factors_cols(fk, sel_t[...], 1.0)
        carried = mm((left * right).astype(BF16), suffix[head_rows(h), :], NN) * fade
        gv = (gv_local[:, cols] + carried).astype(BF16)
        gv_out[:last, cols] = window_value[:last, cols] + gv[:last, :]
        gv_out[last:, cols] = (window_value[last:, cols] + edge[WINDOW:, cols]) + gv[last:, :]
        grad_phi = mm(suffix[head_rows(h), :], faded[:, cols], NT)
        left, right = factors_rows(fk, sel[...], 1.0)
        gfk = gk_local[head_feats(h), :] + feature_grad(grad_phi, left, right, sel_t[...])
        gfk_out[head_feats(h), :] = gfk.astype(BF16)


HBM = pltpu.HBM
VMEM = pltpu.VMEM
NEAR = pl.BlockSpec(memory_space=pltpu.VMEM)
FAR = pl.BlockSpec(memory_space=pltpu.HBM)
ANYWHERE = pl.BlockSpec(memory_space=pl.ANY)
SCALARS = pl.BlockSpec(memory_space=pltpu.SMEM)


def params(mib):
    return pltpu.CompilerParams(vmem_limit_bytes=mib << 20)


def near(*values):
    return [pltpu.with_memory_space_constraint(v, pltpu.VMEM) for v in values]


def far(*values):
    return [pltpu.with_memory_space_constraint(v, pltpu.HBM) for v in values]


def kernel(body, name, ins, outs, mib=8, scratch=()):
    return pl.pallas_call(
        body,
        in_specs=ins,
        out_specs=[NEAR] * len(outs),
        out_shape=outs,
        scratch_shapes=list(scratch),
        compiler_params=params(mib),
        name=name,
    )


def swap(value):
    return lax.all_to_all(value, "seq", split_axis=0, concat_axis=0, tiled=True)


def chain(arrived, reverse):
    return kernel(
        lambda a, o: chain_kernel(reverse, a, o),
        "chain_back" if reverse else "chain_fwd",
        [NEAR],
        [HBM(arrived.shape, BF16)],
        4,
    )(*near(arrived))[0]


def after(value, *others):
    return lax.optimization_barrier((value, *others))


def shifted(value, ways, k):
    return lax.ppermute(value, "mp", [(i, (i + k) % ways) for i in range(ways)])


def body(
    query, key, value, feat_query, feat_key, log_decay, band_width, norm_gain, out_weight, grad_out
):
    count, width = query.shape
    peers = lax.axis_size("seq")
    place = lax.axis_index("seq")
    ways = lax.axis_size("mp")
    lane = lax.axis_index("mp").astype(jnp.int32)[None]
    consts = (jnp.asarray(m) for m in (SEL_K, SEL_K_T, SEL_Q, SEL_Q_T))
    sel_k, sel_kt, sel_q, sel_qt = far(*consts)
    fq_t, fk_t = far(feat_query.T, feat_key.T)
    chunks = (peers, HEADS * ROWS // peers, SIZE)
    states = (HEADS * ROWS, SIZE)
    model = grad_out.shape[1]

    value_arg = value
    state, cum, cum_row, edge, faded, value, key, query = kernel(
        local_state_kernel,
        "local_state",
        [NEAR] * 3 + [FAR] * 3,
        [
            HBM(states, BF16),
            VMEM((count, HEADS), F32),
            VMEM((HEADS, 1, TOK), F32),
            HBM((2 * WINDOW, width), BF16),
            HBM((count, width), BF16),
            VMEM(value.shape, BF16),
            VMEM(key.shape, BF16),
            VMEM(query.shape, BF16),
        ],
        8,
        [pltpu.SemaphoreType.DMA((3,))],
    )(fk_t, *far(log_decay), sel_k, *far(value, key, query))

    arrived = swap(state.reshape(chunks))

    before = lax.ppermute(edge, "seq", [(i, i + 1) for i in range(peers - 1)])
    pieces = [grad_out] + [shifted(grad_out, ways, k) for k in range(1, ways)]

    first_col = jnp.where(place == 0, WINDOW, 0).astype(jnp.int32)[None]
    attended, probs = kernel(
        window_kernel,
        "window",
        [SCALARS] * 2 + [NEAR] * 4,
        [VMEM((count, width), BF16), VMEM((count, width), BF16)],
    )(band_width, first_col, *near(query, key, value, before))

    arrived, attended, probs, *pieces = after(arrived, attended, probs, *pieces)
    chained, fq_late = after(chain(arrived, False), feat_query.T)
    prefix = swap(chained)

    local, phi, phit = kernel(
        intra_kernel,
        "intra",
        [NEAR] * 7,
        [
            VMEM((count, width), F32),
            VMEM((TOK, HEADS * ROWS), BF16),
            VMEM((HEADS * ROWS, TOK), BF16),
        ],
    )(*far(fq_late), fk_t, *near(value, cum, cum_row), sel_q, sel_qt)

    grad, grad_query, win_key, win_value, edge_grad = kernel(
        window_grad_kernel,
        "window_grad",
        [SCALARS] + [NEAR] * 5 + [ANYWHERE] * 4 + [FAR],
        [
            VMEM((count, width), BF16),
            HBM((count, width), BF16),
            HBM((count, width), BF16),
            HBM((count, width), BF16),
            HBM((2 * WINDOW, width), BF16),
        ],
        12,
        [
            pltpu.VMEM((count, model), BF16),
            pltpu.VMEM(out_weight.shape, BF16),
            pltpu.SemaphoreType.DMA((6,)),
        ],
    )(lane, *near(query, key, value, before, probs), *pieces, *far(out_weight))

    prefix, grad, local, phi, phit = after(prefix, grad, local, phi, phit)
    prefix = prefix.reshape(states)

    grad_state, mixed, grad_linear = kernel(
        mix_kernel,
        "mix",
        [NEAR] * 8,
        [HBM(states, BF16), VMEM((count, width), BF16), VMEM((count, width), BF16)],
    )(*near(prefix, phi, phit, local, attended, grad, cum), *far(norm_gain.reshape(1, width)))

    arrived = swap(grad_state.reshape(chunks))

    returned = lax.ppermute(edge_grad, "seq", [(i + 1, i) for i in range(peers - 1)])
    sums = kernel(
        project_kernel,
        "project",
        [SCALARS, NEAR, FAR],
        [HBM((count // ways, model), BF16)] * ways,
        8,
        [
            pltpu.VMEM((count, width), BF16),
            pltpu.VMEM(out_weight.shape, BF16),
            pltpu.SemaphoreType.DMA((ways,)),
        ],
    )(lane, *near(mixed), *far(out_weight))

    arrived, kept = after(arrived, sums[0])
    sums = [kept] + [shifted(sums[k], ways, k) for k in range(1, ways)]
    suffix = swap(chain(arrived, True))

    gq_t, gk_local, gv_local = kernel(
        intra_grad_kernel,
        "intra_grad",
        [NEAR] * 9,
        [
            HBM((HEADS * FEAT, TOK), BF16),
            VMEM((HEADS * FEAT, TOK), F32),
            VMEM((count, width), F32),
        ],
    )(
        fq_t, fk_t, *far(value_arg), *near(cum, cum_row), sel_q, sel_qt,
        *near(prefix, grad_linear),
    )
    layer_out = sum(p.astype(F32) for p in sums).astype(BF16)

    suffix, gk_local, gv_local, layer_out, returned = after(
        suffix, gk_local, gv_local, layer_out, returned
    )

    grad_key, grad_value, gfk_t = kernel(
        finish_kernel,
        "finish",
        [NEAR] * 11,
        [HBM((count, width), BF16), HBM((count, width), BF16), HBM((HEADS * FEAT, TOK), BF16)],
    )(
        fk_t, *near(faded, cum), sel_k, sel_kt,
        *near(suffix.reshape(states), gv_local, gk_local, win_key, win_value, returned),
    )
    return (layer_out, grad_query, grad_key, grad_value, gq_t.T, gfk_t.T)


def solution(mesh):
    return jax.shard_map(
        body,
        mesh=mesh,
        in_specs=(
            P("seq", "mp"),
            P("seq", "mp"),
            P("seq", "mp"),
            P("seq", "mp"),
            P("seq", "mp"),
            P("mp", "seq"),
            P("seq"),
            P("mp"),
            P("mp", None),
            P(("seq", "mp"), None),
        ),
        out_specs=(
            P(("seq", "mp"), None),
            P("seq", "mp"),
            P("seq", "mp"),
            P("seq", "mp"),
            P("seq", "mp"),
            P("seq", "mp"),
        ),
        check_vma=False,
    )
```

```python
import numpy as np
import ml_dtypes
import jax
import jax.numpy as jnp
from jax import lax
from jax.experimental import pallas as pl
from jax.experimental.pallas import tpu as pltpu
from jax.sharding import PartitionSpec as P

WINDOW = 64
EPS = 1e-06
NEG = -1e30
F32 = jnp.float32
BF16 = jnp.bfloat16
TOK = 256
HEADS = 4
SIZE = 128
FEAT = 16
ROWS = 256
SCALE = SIZE**-0.5

NN = (((1,), (0,)), ((), ()))
NT = (((1,), (1,)), ((), ()))
TN = (((0,), (0,)), ((), ()))


def mm(a, b, dims):
    return lax.dot_general(a, b, dims, preferred_element_type=F32)


def selectors(query_side):
    first = np.zeros((ROWS, FEAT), np.float32)
    second = np.zeros_like(first)
    weight = [1 / 32] + [1 / 16] * 7 + [1 / 32, 1 / 4]
    for a in range(FEAT):
        for r in range(10):
            first[a * 16 + r, a] = weight[r] if query_side else 1.0
            if r < 9:
                second[a * 16 + r, (a + r) % FEAT] = 1.0
    both = np.concatenate([first, second], axis=0).astype(ml_dtypes.bfloat16)
    return (both, np.ascontiguousarray(both.T))


SEL_K, SEL_K_T = selectors(False)
SEL_Q, SEL_Q_T = selectors(True)


def row_kind(shape, dim):
    return lax.broadcasted_iota(jnp.int32, shape, dim) % 16


def factors_rows(feats_t, sel, const):
    both = mm(sel, feats_t, NN)
    kind = row_kind((ROWS, 1), 0)
    left = both[:ROWS, :] + jnp.where(kind == 10, const, 0.0)
    right = both[ROWS:, :] + jnp.where((kind == 9) | (kind == 10), 1.0, 0.0)
    return (left, right)


def factors_cols(feats_t, sel_t, const):
    both = mm(feats_t, sel_t, TN)
    kind = row_kind((1, ROWS), 1)
    left = both[:, :ROWS] + jnp.where(kind == 10, const, 0.0)
    right = both[:, ROWS:] + jnp.where((kind == 9) | (kind == 10), 1.0, 0.0)
    return (left, right)


def feature_grad(grad_phi, left, right, sel_t):
    both = jnp.concatenate([grad_phi * right, grad_phi * left], axis=0)
    return mm(sel_t, both.astype(BF16), NN)


def split3(value):
    hi = value.astype(BF16)
    rest = value - hi.astype(F32)
    mid = rest.astype(BF16)
    low = (rest - mid.astype(F32)).astype(BF16)
    return (hi, mid, low)


def with_total(state, total):
    kind = row_kind((ROWS, 1), 0)
    hi, mid, low = split3(total)
    state = jnp.where(kind == 11, hi.astype(F32), state)
    state = jnp.where(kind == 12, mid.astype(F32), state)
    return jnp.where(kind == 13, low.astype(F32), state)


def head_cols(h):
    return slice(h * SIZE, (h + 1) * SIZE)


def head_rows(h):
    return slice(h * ROWS, (h + 1) * ROWS)


def head_feats(h):
    return slice(h * FEAT, (h + 1) * FEAT)


def local_state_kernel(
    feat_t, decay, sel, value_far, key_far, query_far,
    state_out, cum_out, cum_row_out, edge_out, faded_out, value, key, query, sems
):
    first = pltpu.make_async_copy(value_far, value, sems.at[0])
    first.start()
    others = [
        pltpu.make_async_copy(far, near, sems.at[1 + i])
        for i, (far, near) in enumerate(((key_far, key), (query_far, query)))
    ]
    for copy in others:
        copy.start()
    tri = (
        lax.broadcasted_iota(jnp.int32, (TOK, TOK), 0)
        >= lax.broadcasted_iota(jnp.int32, (TOK, TOK), 1)
    ).astype(F32).astype(BF16)
    parts = split3(decay[...])
    cum_row_out[:, 0, :] = sum(mm(p, tri, NT) for p in parts)
    cum_all = sum(mm(tri, p, NT) for p in parts)
    cum_out[...] = cum_all
    first.wait()
    for h in range(HEADS):
        cum = cum_all[:, h : h + 1]
        total = cum[TOK - 1 : TOK, :]
        left, right = factors_rows(feat_t[head_feats(h), :], sel[...], 1.0)
        phi = (left * right).astype(BF16)
        faded = (value[:, head_cols(h)].astype(F32) * jnp.exp(total - cum)).astype(BF16)
        faded_out[:, head_cols(h)] = faded
        state = mm(phi, faded, NN)
        state_out[head_rows(h), :] = with_total(state, total).astype(BF16)
    for copy in others:
        copy.wait()
    edge_out[:WINDOW, :] = key[TOK - WINDOW :, :]
    edge_out[WINDOW:, :] = value[TOK - WINDOW :, :]


def chain_kernel(reverse, arrived, before_out):
    count = arrived.shape[0]
    carry = jnp.zeros((16, SIZE), F32)
    order = range(count)
    for j in reversed(order) if reverse else order:
        before_out[j] = carry.astype(BF16)
        piece = arrived[j].astype(F32)
        total = piece[11:12] + piece[12:13] + piece[13:14]
        carry = carry * jnp.exp(total) + piece


def intra_weights(fq_t, fk_t, cum, cum_row):
    inner = mm(fq_t, fk_t, TN) * FEAT**-0.5
    span = cum - cum_row
    causal = lax.broadcasted_iota(jnp.int32, (TOK, TOK), 0) >= lax.broadcasted_iota(
        jnp.int32, (TOK, TOK), 1
    )
    fade = jnp.where(causal, jnp.exp(jnp.minimum(span, 0.0)), 0.0)
    return (inner, fade, (1.0 + inner + 0.5 * inner * inner) * fade)


def block_pair(before, array, b):
    if b == 0:
        return jnp.concatenate([before, array[:WINDOW, :]], axis=0)
    return array[(b - 1) * WINDOW : (b + 1) * WINDOW, :]


def intra_kernel(fq_t, fk_t, value, cum, cum_row, sel_t, local_out, phi_out):
    for h in range(HEADS):
        feats = fq_t[head_feats(h), :]
        _, _, weights = intra_weights(
            feats, fk_t[head_feats(h), :], cum[:, h : h + 1], cum_row[h]
        )
        local_out[:, head_cols(h)] = mm(weights.astype(BF16), value[:, head_cols(h)], NN)
        left, right = factors_cols(feats, sel_t[...], 1 / 16)
        phi_out[:, head_rows(h)] = (left * right).astype(BF16)


def stacked(parts):
    return jnp.concatenate(parts, axis=0)


def grad_mixed_kernel(
    place, piece0, piece1, piece2, piece3, weight_far, grad_out, rows, weight, sems
):
    pieces = (piece0, piece1, piece2, piece3)
    half = weight.shape[0] // 2
    copies = []
    for k, piece in enumerate(pieces):
        at = ((place[0] + (len(pieces) - k)) % len(pieces)) * WINDOW
        to = rows.at[pl.ds(pl.multiple_of(at, WINDOW), WINDOW), :]
        copies.append(pltpu.make_async_copy(piece, to, sems.at[k]))
    copies.append(pltpu.make_async_copy(weight_far, weight, sems.at[4]))
    for copy in copies:
        copy.start()
    for copy in copies:
        copy.wait()
    for i in range(2):
        part = slice(i * half, (i + 1) * half)
        grad_out[:, part] = mm(rows[...], weight[part, :], NT).astype(BF16)


def window_kernel(band, first_col, query, key, value, before, attended_out, probs_out):
    row = lax.broadcasted_iota(jnp.int32, (WINDOW, 2 * WINDOW), 0)
    col = lax.broadcasted_iota(jnp.int32, (WINDOW, 2 * WINDOW), 1)
    back = WINDOW + row - col
    for b in range(TOK // WINDOW):
        here = slice(b * WINDOW, (b + 1) * WINDOW)
        allowed = (back >= 0) & (back < band[b])
        if b == 0:
            allowed = allowed & (col >= first_col[0])
        scores = []
        for h in range(HEADS):
            cols = head_cols(h)
            keys = block_pair(before[:WINDOW, cols], key.at[:, cols], b)
            scores.append(jnp.where(allowed, mm(query[here, cols], keys, NT) * SCALE, NEG))
        scores = stacked(scores)
        expo = jnp.exp(scores - jnp.max(scores, axis=-1, keepdims=True))
        probs = (expo * (1.0 / jnp.sum(expo, axis=-1, keepdims=True))).astype(BF16)
        for h in range(HEADS):
            cols = head_cols(h)
            mine = probs[h * WINDOW : (h + 1) * WINDOW, :]
            values = block_pair(before[WINDOW:, cols], value.at[:, cols], b)
            probs_out[here, cols] = mine
            attended_out[here, cols] = mm(mine, values, NN).astype(BF16)


def score_grads(probs32, grad_probs):
    grad_probs = grad_probs.astype(BF16).astype(F32)
    along = jnp.sum(probs32 * grad_probs, axis=-1, keepdims=True)
    return (probs32 * (grad_probs - along) * SCALE).astype(BF16)


def edge_grad_kernel(query, value, before, probs, grad, edge_out):
    grads = [grad[:WINDOW, head_cols(h)] for h in range(HEADS)]
    parts = []
    for h in range(HEADS):
        cols = head_cols(h)
        values = block_pair(before[WINDOW:, cols], value.at[:, cols], 0)
        parts.append(mm(grads[h], values, NT))
    probs16 = stacked([probs[:WINDOW, head_cols(h)] for h in range(HEADS)])
    grad_scores = score_grads(probs16.astype(F32), stacked(parts))
    for h in range(HEADS):
        cols = head_cols(h)
        mine = slice(h * WINDOW, (h + 1) * WINDOW)
        key_part = mm(grad_scores[mine, :], query[:WINDOW, cols], TN)
        value_part = mm(probs16[mine, :], grads[h], TN)
        edge_out[:WINDOW, cols] = key_part[:WINDOW, :].astype(BF16)
        edge_out[WINDOW:, cols] = value_part[:WINDOW, :].astype(BF16)


def window_grad_kernel(query, key, value, before, probs, grad, gq_out, gk_out, gv_out):
    blocks = TOK // WINDOW
    for h in range(HEADS):
        cols = head_cols(h)
        keys = [block_pair(before[:WINDOW, cols], key.at[:, cols], b) for b in range(blocks)]
        heres = [slice(b * WINDOW, (b + 1) * WINDOW) for b in range(blocks)]
        grad_probs = stacked(
            [
                mm(
                    grad[heres[b], cols],
                    block_pair(before[WINDOW:, cols], value.at[:, cols], b),
                    NT,
                )
                for b in range(blocks)
            ]
        )
        grad_scores = score_grads(probs[:, cols].astype(F32), grad_probs)
        key_parts = []
        value_parts = []
        for b in range(blocks):
            here = heres[b]
            mine = grad_scores[here, :]
            gq_out[here, cols] = mm(mine, keys[b], NN).astype(BF16)
            key_parts.append(mm(mine, query[here, cols], TN).astype(BF16))
            value_parts.append(mm(probs[here, cols], grad[here, cols], TN).astype(BF16))
        for parts, out in ((key_parts, gk_out), (value_parts, gv_out)):
            for b in range(blocks):
                own = parts[b][WINDOW:, :]
                if b + 1 < blocks:
                    own = own + parts[b + 1][:WINDOW, :]
                out[heres[b], cols] = own


def mix_kernel(
    state, phi, fq_t, sel, local, attended, grad, cum, gain, grad_state_out, mixed_out,
    grad_linear_out
):
    for h in range(HEADS):
        cols = head_cols(h)
        steps = cum[:, h : h + 1]
        fade = jnp.exp(steps)
        linear = local[:, cols] + fade * mm(phi[:, head_rows(h)], state[head_rows(h), :], NN)
        scale = lax.rsqrt(jnp.mean(linear * linear, axis=-1, keepdims=True) + EPS)
        gains = gain[:, cols]
        mixed_out[:, cols] = (
            attended[:, cols].astype(F32) + linear * scale * gains
        ).astype(BF16)
        scaled = grad[:, cols].astype(F32) * gains
        along = jnp.mean(scaled * linear, axis=-1, keepdims=True)
        grad_linear = scale * scaled - linear * (scale * scale * scale * along)
        grad_linear_out[:, cols] = grad_linear.astype(BF16)
        left, right = factors_rows(fq_t[head_feats(h), :], sel[...], 1 / 16)
        phi_t = (left * right).astype(BF16)
        grad_state = mm(phi_t, (grad_linear * fade).astype(BF16), NN)
        total = steps[TOK - 1 : TOK, :]
        grad_state_out[head_rows(h), :] = with_total(grad_state, total).astype(BF16)


def project_kernel(place, mixed, weight_far, piece0, piece1, piece2, piece3, rows, weight, sems):
    pieces = (piece0, piece1, piece2, piece3)
    step = weight.shape[1] // len(pieces)
    parts = [slice(i * step, (i + 1) * step) for i in range(len(pieces))]
    copies = [
        pltpu.make_async_copy(weight_far.at[:, part], weight.at[:, part], sems.at[i])
        for i, part in enumerate(parts)
    ]
    for copy in copies:
        copy.start()
    for k in range(len(pieces)):
        at = ((place[0] + k) % len(pieces)) * WINDOW
        rows[k * WINDOW : (k + 1) * WINDOW, :] = mixed[pl.ds(pl.multiple_of(at, WINDOW), WINDOW), :]
    for copy, part in zip(copies, parts):
        copy.wait()
        product = mm(rows[...], weight[:, part], NN).astype(BF16)
        for k, piece in enumerate(pieces):
            piece[:, part] = product[k * WINDOW : (k + 1) * WINDOW, :]


def intra_grad_kernel(
    fq_t, fk_t, value, cum, cum_row, sel, sel_t, sel_kt, state, grad_linear,
    gq_out, gk_out, gv_out, phi_out
):
    for h in range(HEADS):
        cols = head_cols(h)
        fq, fk, grads = (fq_t[head_feats(h), :], fk_t[head_feats(h), :], grad_linear[:, cols])
        steps = cum[:, h : h + 1]
        inner, fade, weights = intra_weights(fq, fk, steps, cum_row[h])
        gv_out[:, cols] = mm(weights.astype(BF16), grads, TN)
        grad_inner = mm(grads, value[:, cols], NT) * fade * (1.0 + inner) * FEAT**-0.5
        grad_inner = grad_inner.astype(BF16)
        gk_out[head_feats(h), :] = mm(fq, grad_inner, NN)
        faded = (grads.astype(F32) * jnp.exp(steps)).astype(BF16)
        grad_phi = mm(state[head_rows(h), :], faded, NT)
        left, right = factors_rows(fq, sel[...], 1 / 16)
        gq = mm(fk, grad_inner, NT) + feature_grad(grad_phi, left, right, sel_t[...])
        gq_out[head_feats(h), :] = gq.astype(BF16)
        left, right = factors_cols(fk, sel_kt[...], 1.0)
        phi_out[:, head_rows(h)] = (left * right).astype(BF16)


def finish_kernel(
    fk_t, phi, faded, cum, sel, sel_t, suffix, gv_local, gk_local, window_key, window_value, edge,
    gk_out, gv_out, gfk_out
):
    last = TOK - WINDOW
    gk_out[:last, :] = window_key[:last, :]
    gk_out[last:, :] = window_key[last:, :] + edge[:WINDOW, :]
    for h in range(HEADS):
        cols = head_cols(h)
        fk = fk_t[head_feats(h), :]
        steps = cum[:, h : h + 1]
        fade = jnp.exp(steps[TOK - 1 : TOK, :] - steps)
        carried = mm(phi[:, head_rows(h)], suffix[head_rows(h), :], NN) * fade
        gv = (gv_local[:, cols] + carried).astype(BF16)
        gv_out[:last, cols] = window_value[:last, cols] + gv[:last, :]
        gv_out[last:, cols] = (window_value[last:, cols] + edge[WINDOW:, cols]) + gv[last:, :]
        grad_phi = mm(suffix[head_rows(h), :], faded[:, cols], NT)
        left, right = factors_rows(fk, sel[...], 1.0)
        gfk = gk_local[head_feats(h), :] + feature_grad(grad_phi, left, right, sel_t[...])
        gfk_out[head_feats(h), :] = gfk.astype(BF16)


HBM = pltpu.HBM
EARLY = (2,)
VMEM = pltpu.VMEM
NEAR = pl.BlockSpec(memory_space=pltpu.VMEM)
FAR = pl.BlockSpec(memory_space=pltpu.HBM)
ANYWHERE = pl.BlockSpec(memory_space=pl.ANY)
SCALARS = pl.BlockSpec(memory_space=pltpu.SMEM)


def params(mib):
    return pltpu.CompilerParams(vmem_limit_bytes=mib << 20)


def near(*values):
    return [pltpu.with_memory_space_constraint(jnp.asarray(v), pltpu.VMEM) for v in values]


def far(*values):
    return [pltpu.with_memory_space_constraint(v, pltpu.HBM) for v in values]


def kernel(body, name, ins, outs, mib=8, scratch=()):
    return pl.pallas_call(
        body,
        in_specs=ins,
        out_specs=[NEAR] * len(outs),
        out_shape=outs,
        scratch_shapes=list(scratch),
        compiler_params=params(mib),
        name=name,
    )


def swap(value):
    return lax.all_to_all(value, "seq", split_axis=0, concat_axis=0, tiled=True)


def chain(arrived, reverse):
    return kernel(
        lambda a, o: chain_kernel(reverse, a, o),
        "chain_back" if reverse else "chain_fwd",
        [NEAR],
        [HBM(arrived.shape, BF16)],
        4,
    )(*near(arrived))[0]


def after(value, *others):
    return lax.optimization_barrier((value, *others))


def shifted(value, ways, k):
    return lax.ppermute(value, "mp", [(i, (i + k) % ways) for i in range(ways)])


def body(
    query, key, value, feat_query, feat_key, log_decay, band_width, norm_gain, out_weight, grad_out
):
    count, width = query.shape
    peers = lax.axis_size("seq")
    place = lax.axis_index("seq")
    ways = lax.axis_size("mp")
    lane = lax.axis_index("mp").astype(jnp.int32)[None]
    consts = (jnp.asarray(m) for m in (SEL_K, SEL_K_T, SEL_Q, SEL_Q_T))
    sel_k, sel_kt, sel_q, sel_qt = far(*consts)
    fq_t, fk_t = far(feat_query.T, feat_key.T)
    chunks = (peers, HEADS * ROWS // peers, SIZE)
    states = (HEADS * ROWS, SIZE)
    model = grad_out.shape[1]

    value_arg, args = (value, (query, key, value))
    state, cum, cum_row, edge, faded, value, key, query = kernel(
        local_state_kernel,
        "local_state",
        [NEAR] * 3 + [FAR] * 3,
        [
            HBM(states, BF16),
            VMEM((count, HEADS), F32),
            VMEM((HEADS, 1, TOK), F32),
            HBM((2 * WINDOW, width), BF16),
            HBM((count, width), BF16),
            VMEM(value.shape, BF16),
            VMEM(key.shape, BF16),
            VMEM(query.shape, BF16),
        ],
        8,
        [pltpu.SemaphoreType.DMA((3,))],
    )(fk_t, *far(log_decay), sel_k, *far(value, key, query))

    arrived = swap(state.reshape(chunks))

    before = lax.ppermute(edge, "seq", [(i, i + 1) for i in range(peers - 1)])
    pieces = [grad_out] + [shifted(grad_out, ways, k) for k in range(1, ways)]

    arrived, before, *early = after(arrived, before, *(pieces[k] for k in EARLY))
    for k, piece in zip(EARLY, early):
        pieces[k] = piece
    chained, before, fq_late = after(chain(arrived, False), before, feat_query.T)
    prefix = swap(chained)

    local, phi = kernel(
        intra_kernel,
        "intra",
        [NEAR] * 6,
        [VMEM((count, width), F32), VMEM((TOK, HEADS * ROWS), BF16)],
    )(*far(fq_late), fk_t, *near(value, cum, cum_row), sel_qt)

    first_col = jnp.where(place == 0, WINDOW, 0).astype(jnp.int32)[None]
    attended, probs = kernel(
        window_kernel,
        "window",
        [SCALARS] * 2 + [NEAR] * 4,
        [VMEM((count, width), BF16)] * 2,
    )(band_width, first_col, *near(query, key, value, before))
    grad = kernel(
        grad_mixed_kernel,
        "grad_mixed",
        [SCALARS] + [FAR] * 5,
        [VMEM((count, width), BF16)],
        12,
        [
            pltpu.VMEM((count, model), BF16),
            pltpu.VMEM(out_weight.shape, BF16),
            pltpu.SemaphoreType.DMA((5,)),
        ],
    )(lane, *far(*pieces, out_weight))[0]

    prefix, attended, probs, grad, local, phi = after(
        prefix, attended, probs, grad, local, phi
    )
    prefix = prefix.reshape(states)

    grad_state, mixed, grad_linear = kernel(
        mix_kernel,
        "mix",
        [NEAR] * 9,
        [HBM(states, BF16), VMEM((count, width), BF16), VMEM((count, width), BF16)],
    )(*near(prefix, phi, feat_query.T, SEL_Q, local, attended, grad, cum, norm_gain.reshape(1, width)))

    grad_state, probs = after(grad_state, probs)
    arrived = swap(grad_state.reshape(chunks))

    sums = kernel(
        project_kernel,
        "project",
        [SCALARS, NEAR, FAR],
        [HBM((count // ways, model), BF16)] * ways,
        8,
        [
            pltpu.VMEM((count, width), BF16),
            pltpu.VMEM(out_weight.shape, BF16),
            pltpu.SemaphoreType.DMA((ways,)),
        ],
    )(lane, *near(mixed), *far(out_weight))

    arrived, kept = after(arrived, sums[0])
    sums = [kept] + [shifted(sums[k], ways, k) for k in range(1, ways)]
    chained, probs = after(chain(arrived, True), probs)
    suffix = swap(chained)

    edge_grad = kernel(
        edge_grad_kernel,
        "edge_grad",
        [NEAR] * 5,
        [HBM((2 * WINDOW, width), BF16)],
    )(*far(args[0], args[2]), *near(before, probs, grad))[0]
    returned = lax.ppermute(edge_grad, "seq", [(i + 1, i) for i in range(peers - 1)])
    edge_grad, probs = after(edge_grad, probs)
    grad_query, win_key, win_value = kernel(
        window_grad_kernel,
        "window_grad",
        [NEAR] * 6,
        [HBM((count, width), BF16), VMEM((count, width), BF16), VMEM((count, width), BF16)],
    )(*far(*args), *near(before, probs, grad))

    gq_t, gk_local, gv_local, phi_k = kernel(
        intra_grad_kernel,
        "intra_grad",
        [NEAR] * 10,
        [
            HBM((HEADS * FEAT, TOK), BF16),
            VMEM((HEADS * FEAT, TOK), F32),
            VMEM((count, width), F32),
            VMEM((TOK, HEADS * ROWS), BF16),
        ],
    )(
        fq_t, fk_t, *far(value_arg), *near(cum, cum_row), sel_q, sel_qt, sel_kt,
        *near(prefix, grad_linear),
    )
    layer_out = sum(p.astype(F32) for p in sums).astype(BF16)

    suffix, gk_local, gv_local, phi_k, layer_out, returned, win_key, win_value = after(
        suffix, gk_local, gv_local, phi_k, layer_out, returned, win_key, win_value
    )

    grad_key, grad_value, gfk_t = kernel(
        finish_kernel,
        "finish",
        [NEAR] * 12,
        [HBM((count, width), BF16), HBM((count, width), BF16), HBM((HEADS * FEAT, TOK), BF16)],
    )(
        *near(feat_key.T, phi_k, faded, cum, SEL_K, SEL_K_T),
        *near(suffix.reshape(states), gv_local, gk_local, win_key, win_value, returned),
    )
    return (layer_out, grad_query, grad_key, grad_value, gq_t.T, gfk_t.T)


def solution(mesh):
    return jax.shard_map(
        body,
        mesh=mesh,
        in_specs=(
            P("seq", "mp"),
            P("seq", "mp"),
            P("seq", "mp"),
            P("seq", "mp"),
            P("seq", "mp"),
            P("mp", "seq"),
            P("seq"),
            P("mp"),
            P("mp", None),
            P(("seq", "mp"), None),
        ),
        out_specs=(
            P(("seq", "mp"), None),
            P("seq", "mp"),
            P("seq", "mp"),
            P("seq", "mp"),
            P("seq", "mp"),
            P("seq", "mp"),
        ),
        check_vma=False,
    )
```

```python
import numpy as np
import ml_dtypes
import jax
import jax.numpy as jnp
from jax import lax
from jax.experimental import pallas as pl
from jax.experimental.pallas import tpu as pltpu
from jax.sharding import PartitionSpec as P

WINDOW = 64
EPS = 1e-06
NEG = -1e30
F32 = jnp.float32
BF16 = jnp.bfloat16
TOK = 256
HEADS = 4
SIZE = 128
FEAT = 16
ROWS = 256
SCALE = SIZE**-0.5

NN = (((1,), (0,)), ((), ()))
NT = (((1,), (1,)), ((), ()))
TN = (((0,), (0,)), ((), ()))


def mm(a, b, dims):
    return lax.dot_general(a, b, dims, preferred_element_type=F32)


def selectors(query_side):
    first = np.zeros((ROWS, FEAT), np.float32)
    second = np.zeros_like(first)
    weight = [1 / 32] + [1 / 16] * 7 + [1 / 32, 1 / 4]
    for a in range(FEAT):
        for r in range(10):
            first[a * 16 + r, a] = weight[r] if query_side else 1.0
            if r < 9:
                second[a * 16 + r, (a + r) % FEAT] = 1.0
    both = np.concatenate([first, second], axis=0).astype(ml_dtypes.bfloat16)
    return (both, np.ascontiguousarray(both.T))


SEL_K, SEL_K_T = selectors(False)
SEL_Q, SEL_Q_T = selectors(True)


def row_kind(shape, dim):
    return lax.broadcasted_iota(jnp.int32, shape, dim) % 16


def factors_rows(feats_t, sel, const):
    both = mm(sel, feats_t, NN)
    kind = row_kind((ROWS, 1), 0)
    left = both[:ROWS, :] + jnp.where(kind == 10, const, 0.0)
    right = both[ROWS:, :] + jnp.where((kind == 9) | (kind == 10), 1.0, 0.0)
    return (left, right)


def factors_cols(feats_t, sel_t, const):
    both = mm(feats_t, sel_t, TN)
    kind = row_kind((1, ROWS), 1)
    left = both[:, :ROWS] + jnp.where(kind == 10, const, 0.0)
    right = both[:, ROWS:] + jnp.where((kind == 9) | (kind == 10), 1.0, 0.0)
    return (left, right)


def feature_grad(grad_phi, left, right, sel_t):
    both = jnp.concatenate([grad_phi * right, grad_phi * left], axis=0)
    return mm(sel_t, both.astype(BF16), NN)


def split3(value):
    hi = value.astype(BF16)
    rest = value - hi.astype(F32)
    mid = rest.astype(BF16)
    low = (rest - mid.astype(F32)).astype(BF16)
    return (hi, mid, low)


def with_total(state, total):
    kind = row_kind((ROWS, 1), 0)
    hi, mid, low = split3(total)
    state = jnp.where(kind == 11, hi.astype(F32), state)
    state = jnp.where(kind == 12, mid.astype(F32), state)
    return jnp.where(kind == 13, low.astype(F32), state)


def head_cols(h):
    return slice(h * SIZE, (h + 1) * SIZE)


def head_rows(h):
    return slice(h * ROWS, (h + 1) * ROWS)


def head_feats(h):
    return slice(h * FEAT, (h + 1) * FEAT)


def local_state_kernel(
    feat_t, decay, sel, value_far, key_far, query_far,
    state_out, cum_out, cum_row_out, edge_out, faded_out, value, key, query, sems
):
    first = pltpu.make_async_copy(value_far, value, sems.at[0])
    first.start()
    others = [
        pltpu.make_async_copy(far, near, sems.at[1 + i])
        for i, (far, near) in enumerate(((key_far, key), (query_far, query)))
    ]
    for copy in others:
        copy.start()
    tri = (
        lax.broadcasted_iota(jnp.int32, (TOK, TOK), 0)
        >= lax.broadcasted_iota(jnp.int32, (TOK, TOK), 1)
    ).astype(F32).astype(BF16)
    parts = split3(decay[...])
    cum_row_out[:, 0, :] = sum(mm(p, tri, NT) for p in parts)
    cum_all = sum(mm(tri, p, NT) for p in parts)
    cum_out[...] = cum_all
    first.wait()
    for h in range(HEADS):
        cum = cum_all[:, h : h + 1]
        total = cum[TOK - 1 : TOK, :]
        left, right = factors_rows(feat_t[head_feats(h), :], sel[...], 1.0)
        phi = (left * right).astype(BF16)
        faded = (value[:, head_cols(h)].astype(F32) * jnp.exp(total - cum)).astype(BF16)
        faded_out[:, head_cols(h)] = faded
        state = mm(phi, faded, NN)
        state_out[head_rows(h), :] = with_total(state, total).astype(BF16)
    for copy in others:
        copy.wait()
    edge_out[:WINDOW, :] = key[TOK - WINDOW :, :]
    edge_out[WINDOW:, :] = value[TOK - WINDOW :, :]


def chain_kernel(reverse, arrived, before_out):
    count = arrived.shape[0]
    carry = jnp.zeros((16, SIZE), F32)
    order = range(count)
    for j in reversed(order) if reverse else order:
        before_out[j] = carry.astype(BF16)
        piece = arrived[j].astype(F32)
        total = piece[11:12] + piece[12:13] + piece[13:14]
        carry = carry * jnp.exp(total) + piece


def intra_weights(fq_t, fk_t, cum, cum_row):
    inner = mm(fq_t, fk_t, TN) * FEAT**-0.5
    span = cum - cum_row
    causal = lax.broadcasted_iota(jnp.int32, (TOK, TOK), 0) >= lax.broadcasted_iota(
        jnp.int32, (TOK, TOK), 1
    )
    fade = jnp.where(causal, jnp.exp(jnp.minimum(span, 0.0)), 0.0)
    return (inner, fade, (1.0 + inner + 0.5 * inner * inner) * fade)


def block_pair(before, array, b):
    if b == 0:
        return jnp.concatenate([before, array[:WINDOW, :]], axis=0)
    return array[(b - 1) * WINDOW : (b + 1) * WINDOW, :]


def intra_kernel(fq_t, fk_t, value, cum, cum_row, sel_t, local_out, phi_out):
    for h in range(HEADS):
        feats = fq_t[head_feats(h), :]
        _, _, weights = intra_weights(
            feats, fk_t[head_feats(h), :], cum[:, h : h + 1], cum_row[h]
        )
        local_out[:, head_cols(h)] = mm(weights.astype(BF16), value[:, head_cols(h)], NN)
        left, right = factors_cols(feats, sel_t[...], 1 / 16)
        phi_out[:, head_rows(h)] = (left * right).astype(BF16)


def stacked(parts):
    return jnp.concatenate(parts, axis=0)


def rows_of(lane, ways, k):
    return pl.ds(pl.multiple_of(((lane + (ways - k)) % ways) * WINDOW, WINDOW), WINDOW)


def grad_mixed_kernel(place, piece1, piece3, weight, early, grad_out, rows, sems):
    ways = grad_out.shape[0] // WINDOW
    copies = [
        pltpu.make_async_copy(piece, rows.at[i * WINDOW : (i + 1) * WINDOW, :], sems.at[i])
        for i, piece in enumerate((piece1, piece3))
    ]
    for copy in copies:
        copy.start()
    for i, k in enumerate((0, 2)):
        grad_out[rows_of(place[0], ways, k), :] = early[i * WINDOW : (i + 1) * WINDOW, :]
    for copy in copies:
        copy.wait()
    grad = mm(rows[...], weight[...], NT).astype(BF16)
    for i, k in enumerate((1, 3)):
        grad_out[rows_of(place[0], ways, k), :] = grad[i * WINDOW : (i + 1) * WINDOW, :]


def window_kernel(
    band, first_col, query, key, value, before, own, piece2, weight_far,
    attended_out, probs_out, grad_out, weight, rows, sems
):
    copies = [
        pltpu.make_async_copy(own, rows.at[:WINDOW, :], sems.at[0]),
        pltpu.make_async_copy(piece2, rows.at[WINDOW:, :], sems.at[1]),
        pltpu.make_async_copy(weight_far, weight, sems.at[2]),
    ]
    for copy in copies:
        copy.start()
    row = lax.broadcasted_iota(jnp.int32, (WINDOW, 2 * WINDOW), 0)
    col = lax.broadcasted_iota(jnp.int32, (WINDOW, 2 * WINDOW), 1)
    back = WINDOW + row - col
    for b in range(TOK // WINDOW):
        here = slice(b * WINDOW, (b + 1) * WINDOW)
        allowed = (back >= 0) & (back < band[b])
        if b == 0:
            allowed = allowed & (col >= first_col[0])
        scores = []
        for h in range(HEADS):
            cols = head_cols(h)
            keys = block_pair(before[:WINDOW, cols], key.at[:, cols], b)
            scores.append(jnp.where(allowed, mm(query[here, cols], keys, NT) * SCALE, NEG))
        scores = stacked(scores)
        expo = jnp.exp(scores - jnp.max(scores, axis=-1, keepdims=True))
        probs = (expo * (1.0 / jnp.sum(expo, axis=-1, keepdims=True))).astype(BF16)
        for h in range(HEADS):
            cols = head_cols(h)
            mine = probs[h * WINDOW : (h + 1) * WINDOW, :]
            values = block_pair(before[WINDOW:, cols], value.at[:, cols], b)
            probs_out[here, cols] = mine
            attended_out[here, cols] = mm(mine, values, NN).astype(BF16)
    for copy in copies:
        copy.wait()
    grad_out[...] = mm(rows[...], weight[...], NT).astype(BF16)


def score_grads(probs32, grad_probs):
    grad_probs = grad_probs.astype(BF16).astype(F32)
    along = jnp.sum(probs32 * grad_probs, axis=-1, keepdims=True)
    return (probs32 * (grad_probs - along) * SCALE).astype(BF16)


def edge_grad_kernel(query, value, before, probs, grad, edge_out):
    grads = [grad[:WINDOW, head_cols(h)] for h in range(HEADS)]
    parts = []
    for h in range(HEADS):
        cols = head_cols(h)
        values = block_pair(before[WINDOW:, cols], value.at[:, cols], 0)
        parts.append(mm(grads[h], values, NT))
    probs16 = stacked([probs[:WINDOW, head_cols(h)] for h in range(HEADS)])
    grad_scores = score_grads(probs16.astype(F32), stacked(parts))
    for h in range(HEADS):
        cols = head_cols(h)
        mine = slice(h * WINDOW, (h + 1) * WINDOW)
        key_part = mm(grad_scores[mine, :], query[:WINDOW, cols], TN)
        value_part = mm(probs16[mine, :], grads[h], TN)
        edge_out[:WINDOW, cols] = key_part[:WINDOW, :].astype(BF16)
        edge_out[WINDOW:, cols] = value_part[:WINDOW, :].astype(BF16)


def window_grad_kernel(query, key, value, before, probs, grad, gq_out, gk_out, gv_out):
    blocks = TOK // WINDOW
    for h in range(HEADS):
        cols = head_cols(h)
        keys = [block_pair(before[:WINDOW, cols], key.at[:, cols], b) for b in range(blocks)]
        heres = [slice(b * WINDOW, (b + 1) * WINDOW) for b in range(blocks)]
        grad_probs = stacked(
            [
                mm(
                    grad[heres[b], cols],
                    block_pair(before[WINDOW:, cols], value.at[:, cols], b),
                    NT,
                )
                for b in range(blocks)
            ]
        )
        grad_scores = score_grads(probs[:, cols].astype(F32), grad_probs)
        key_parts = []
        value_parts = []
        for b in range(blocks):
            here = heres[b]
            mine = grad_scores[here, :]
            gq_out[here, cols] = mm(mine, keys[b], NN).astype(BF16)
            key_parts.append(mm(mine, query[here, cols], TN).astype(BF16))
            value_parts.append(mm(probs[here, cols], grad[here, cols], TN).astype(BF16))
        for parts, out in ((key_parts, gk_out), (value_parts, gv_out)):
            for b in range(blocks):
                own = parts[b][WINDOW:, :]
                if b + 1 < blocks:
                    own = own + parts[b + 1][:WINDOW, :]
                out[heres[b], cols] = own


def mix_kernel(
    state, phi, fq_t, sel, local, attended, grad, cum, gain, grad_state_out, mixed_out,
    grad_linear_out
):
    for h in range(HEADS):
        cols = head_cols(h)
        steps = cum[:, h : h + 1]
        fade = jnp.exp(steps)
        linear = local[:, cols] + fade * mm(phi[:, head_rows(h)], state[head_rows(h), :], NN)
        scale = lax.rsqrt(jnp.mean(linear * linear, axis=-1, keepdims=True) + EPS)
        gains = gain[:, cols]
        mixed_out[:, cols] = (
            attended[:, cols].astype(F32) + linear * scale * gains
        ).astype(BF16)
        scaled = grad[:, cols].astype(F32) * gains
        along = jnp.mean(scaled * linear, axis=-1, keepdims=True)
        grad_linear = scale * scaled - linear * (scale * scale * scale * along)
        grad_linear_out[:, cols] = grad_linear.astype(BF16)
        left, right = factors_rows(fq_t[head_feats(h), :], sel[...], 1 / 16)
        phi_t = (left * right).astype(BF16)
        grad_state = mm(phi_t, (grad_linear * fade).astype(BF16), NN)
        total = steps[TOK - 1 : TOK, :]
        grad_state_out[head_rows(h), :] = with_total(grad_state, total).astype(BF16)


def project_kernel(place, mixed, weight_far, piece0, piece1, piece2, piece3, rows, weight, sems):
    pieces = (piece0, piece1, piece2, piece3)
    step = weight.shape[1] // len(pieces)
    parts = [slice(i * step, (i + 1) * step) for i in range(len(pieces))]
    copies = [
        pltpu.make_async_copy(weight_far.at[:, part], weight.at[:, part], sems.at[i])
        for i, part in enumerate(parts)
    ]
    for copy in copies:
        copy.start()
    for k in range(len(pieces)):
        at = ((place[0] + k) % len(pieces)) * WINDOW
        rows[k * WINDOW : (k + 1) * WINDOW, :] = mixed[pl.ds(pl.multiple_of(at, WINDOW), WINDOW), :]
    for copy, part in zip(copies, parts):
        copy.wait()
        product = mm(rows[...], weight[:, part], NN).astype(BF16)
        for k, piece in enumerate(pieces):
            piece[:, part] = product[k * WINDOW : (k + 1) * WINDOW, :]


def intra_grad_kernel(
    fq_t, fk_t, value, cum, cum_row, sel, sel_t, sel_kt, state, grad_linear,
    gq_out, gk_out, gv_out, phi_out
):
    for h in range(HEADS):
        cols = head_cols(h)
        fq, fk, grads = (fq_t[head_feats(h), :], fk_t[head_feats(h), :], grad_linear[:, cols])
        steps = cum[:, h : h + 1]
        inner, fade, weights = intra_weights(fq, fk, steps, cum_row[h])
        gv_out[:, cols] = mm(weights.astype(BF16), grads, TN)
        grad_inner = mm(grads, value[:, cols], NT) * fade * (1.0 + inner) * FEAT**-0.5
        grad_inner = grad_inner.astype(BF16)
        gk_out[head_feats(h), :] = mm(fq, grad_inner, NN)
        faded = (grads.astype(F32) * jnp.exp(steps)).astype(BF16)
        grad_phi = mm(state[head_rows(h), :], faded, NT)
        left, right = factors_rows(fq, sel[...], 1 / 16)
        gq = mm(fk, grad_inner, NT) + feature_grad(grad_phi, left, right, sel_t[...])
        gq_out[head_feats(h), :] = gq.astype(BF16)
        left, right = factors_cols(fk, sel_kt[...], 1.0)
        phi_out[:, head_rows(h)] = (left * right).astype(BF16)


def finish_kernel(
    fk_t, phi, faded, cum, sel, sel_t, suffix, gv_local, gk_local, window_key, window_value, edge,
    gk_out, gv_out, gfk_out
):
    last = TOK - WINDOW
    gk_out[:last, :] = window_key[:last, :]
    gk_out[last:, :] = window_key[last:, :] + edge[:WINDOW, :]
    for h in range(HEADS):
        cols = head_cols(h)
        fk = fk_t[head_feats(h), :]
        steps = cum[:, h : h + 1]
        fade = jnp.exp(steps[TOK - 1 : TOK, :] - steps)
        carried = mm(phi[:, head_rows(h)], suffix[head_rows(h), :], NN) * fade
        gv = (gv_local[:, cols] + carried).astype(BF16)
        gv_out[:last, cols] = window_value[:last, cols] + gv[:last, :]
        gv_out[last:, cols] = (window_value[last:, cols] + edge[WINDOW:, cols]) + gv[last:, :]
        grad_phi = mm(suffix[head_rows(h), :], faded[:, cols], NT)
        left, right = factors_rows(fk, sel[...], 1.0)
        gfk = gk_local[head_feats(h), :] + feature_grad(grad_phi, left, right, sel_t[...])
        gfk_out[head_feats(h), :] = gfk.astype(BF16)


HBM = pltpu.HBM
EARLY = (2,)
VMEM = pltpu.VMEM
NEAR = pl.BlockSpec(memory_space=pltpu.VMEM)
FAR = pl.BlockSpec(memory_space=pltpu.HBM)
ANYWHERE = pl.BlockSpec(memory_space=pl.ANY)
SCALARS = pl.BlockSpec(memory_space=pltpu.SMEM)


def params(mib):
    return pltpu.CompilerParams(vmem_limit_bytes=mib << 20)


def near(*values):
    return [pltpu.with_memory_space_constraint(jnp.asarray(v), pltpu.VMEM) for v in values]


def far(*values):
    return [pltpu.with_memory_space_constraint(v, pltpu.HBM) for v in values]


def kernel(body, name, ins, outs, mib=8, scratch=()):
    return pl.pallas_call(
        body,
        in_specs=ins,
        out_specs=[NEAR] * len(outs),
        out_shape=outs,
        scratch_shapes=list(scratch),
        compiler_params=params(mib),
        name=name,
    )


def swap(value):
    return lax.all_to_all(value, "seq", split_axis=0, concat_axis=0, tiled=True)


def chain(arrived, reverse):
    return kernel(
        lambda a, o: chain_kernel(reverse, a, o),
        "chain_back" if reverse else "chain_fwd",
        [NEAR],
        [HBM(arrived.shape, BF16)],
        4,
    )(*near(arrived))[0]


def after(value, *others):
    return lax.optimization_barrier((value, *others))


def shifted(value, ways, k):
    return lax.ppermute(value, "mp", [(i, (i + k) % ways) for i in range(ways)])


def body(
    query, key, value, feat_query, feat_key, log_decay, band_width, norm_gain, out_weight, grad_out
):
    count, width = query.shape
    peers = lax.axis_size("seq")
    place = lax.axis_index("seq")
    ways = lax.axis_size("mp")
    lane = lax.axis_index("mp").astype(jnp.int32)[None]
    consts = (jnp.asarray(m) for m in (SEL_K, SEL_K_T, SEL_Q, SEL_Q_T))
    sel_k, sel_kt, sel_q, sel_qt = far(*consts)
    fq_t, fk_t = far(feat_query.T, feat_key.T)
    chunks = (peers, HEADS * ROWS // peers, SIZE)
    states = (HEADS * ROWS, SIZE)
    model = grad_out.shape[1]

    value_arg, args = (value, (query, key, value))
    state, cum, cum_row, edge, faded, value, key, query = kernel(
        local_state_kernel,
        "local_state",
        [NEAR] * 3 + [FAR] * 3,
        [
            HBM(states, BF16),
            VMEM((count, HEADS), F32),
            VMEM((HEADS, 1, TOK), F32),
            HBM((2 * WINDOW, width), BF16),
            HBM((count, width), BF16),
            VMEM(value.shape, BF16),
            VMEM(key.shape, BF16),
            VMEM(query.shape, BF16),
        ],
        8,
        [pltpu.SemaphoreType.DMA((3,))],
    )(fk_t, *far(log_decay), sel_k, *far(value, key, query))

    arrived = swap(state.reshape(chunks))

    before = lax.ppermute(edge, "seq", [(i, i + 1) for i in range(peers - 1)])
    pieces = [grad_out] + [shifted(grad_out, ways, k) for k in range(1, ways)]

    arrived, before, *early = after(arrived, before, *(pieces[k] for k in EARLY))
    for k, piece in zip(EARLY, early):
        pieces[k] = piece
    chained, before, fq_late = after(chain(arrived, False), before, feat_query.T)
    prefix = swap(chained)

    local, phi = kernel(
        intra_kernel,
        "intra",
        [NEAR] * 6,
        [VMEM((count, width), F32), VMEM((TOK, HEADS * ROWS), BF16)],
    )(*far(fq_late), fk_t, *near(value, cum, cum_row), sel_qt)

    first_col = jnp.where(place == 0, WINDOW, 0).astype(jnp.int32)[None]
    attended, probs, grad_early, weight = kernel(
        window_kernel,
        "window",
        [SCALARS] * 2 + [NEAR] * 4 + [FAR] * 3,
        [VMEM((count, width), BF16)] * 2
        + [VMEM((2 * WINDOW, width), BF16), VMEM(out_weight.shape, BF16)],
        8,
        [pltpu.VMEM((2 * WINDOW, model), BF16), pltpu.SemaphoreType.DMA((3,))],
    )(
        band_width, first_col, *near(query, key, value, before),
        *far(grad_out, pieces[2], out_weight),
    )
    grad = kernel(
        grad_mixed_kernel,
        "grad_mixed",
        [SCALARS] + [FAR] * 2 + [NEAR] * 2,
        [VMEM((count, width), BF16)],
        8,
        [pltpu.VMEM((2 * WINDOW, model), BF16), pltpu.SemaphoreType.DMA((2,))],
    )(lane, *far(pieces[1], pieces[3]), *near(weight, grad_early))[0]

    prefix, attended, probs, grad, local, phi = after(
        prefix, attended, probs, grad, local, phi
    )
    prefix = prefix.reshape(states)

    grad_state, mixed, grad_linear = kernel(
        mix_kernel,
        "mix",
        [NEAR] * 9,
        [HBM(states, BF16), VMEM((count, width), BF16), VMEM((count, width), BF16)],
    )(*near(prefix, phi, feat_query.T, SEL_Q, local, attended, grad, cum, norm_gain.reshape(1, width)))

    grad_state, probs = after(grad_state, probs)
    arrived = swap(grad_state.reshape(chunks))

    sums = kernel(
        project_kernel,
        "project",
        [SCALARS, NEAR, FAR],
        [HBM((count // ways, model), BF16)] * ways,
        8,
        [
            pltpu.VMEM((count, width), BF16),
            pltpu.VMEM(out_weight.shape, BF16),
            pltpu.SemaphoreType.DMA((ways,)),
        ],
    )(lane, *near(mixed), *far(out_weight))

    arrived, kept = after(arrived, sums[0])
    sums = [kept] + [shifted(sums[k], ways, k) for k in range(1, ways)]
    chained, probs = after(chain(arrived, True), probs)
    suffix = swap(chained)

    edge_grad = kernel(
        edge_grad_kernel,
        "edge_grad",
        [NEAR] * 5,
        [HBM((2 * WINDOW, width), BF16)],
    )(*far(args[0], args[2]), *near(before, probs, grad))[0]
    returned = lax.ppermute(edge_grad, "seq", [(i + 1, i) for i in range(peers - 1)])
    edge_grad, probs = after(edge_grad, probs)
    grad_query, win_key, win_value = kernel(
        window_grad_kernel,
        "window_grad",
        [NEAR] * 6,
        [HBM((count, width), BF16), VMEM((count, width), BF16), VMEM((count, width), BF16)],
    )(*far(*args), *near(before, probs, grad))

    gq_t, gk_local, gv_local, phi_k = kernel(
        intra_grad_kernel,
        "intra_grad",
        [NEAR] * 10,
        [
            HBM((HEADS * FEAT, TOK), BF16),
            VMEM((HEADS * FEAT, TOK), F32),
            VMEM((count, width), F32),
            VMEM((TOK, HEADS * ROWS), BF16),
        ],
    )(
        fq_t, fk_t, *far(value_arg), *near(cum, cum_row), sel_q, sel_qt, sel_kt,
        *near(prefix, grad_linear),
    )
    layer_out = sum(p.astype(F32) for p in sums).astype(BF16)

    suffix, gk_local, gv_local, phi_k, layer_out, returned, win_key, win_value = after(
        suffix, gk_local, gv_local, phi_k, layer_out, returned, win_key, win_value
    )

    grad_key, grad_value, gfk_t = kernel(
        finish_kernel,
        "finish",
        [NEAR] * 12,
        [HBM((count, width), BF16), HBM((count, width), BF16), HBM((HEADS * FEAT, TOK), BF16)],
    )(
        *near(feat_key.T, phi_k, faded, cum, SEL_K, SEL_K_T),
        *near(suffix.reshape(states), gv_local, gk_local, win_key, win_value, returned),
    )
    return (layer_out, grad_query, grad_key, grad_value, gq_t.T, gfk_t.T)


def solution(mesh):
    return jax.shard_map(
        body,
        mesh=mesh,
        in_specs=(
            P("seq", "mp"),
            P("seq", "mp"),
            P("seq", "mp"),
            P("seq", "mp"),
            P("seq", "mp"),
            P("mp", "seq"),
            P("seq"),
            P("mp"),
            P("mp", None),
            P(("seq", "mp"), None),
        ),
        out_specs=(
            P(("seq", "mp"), None),
            P("seq", "mp"),
            P("seq", "mp"),
            P("seq", "mp"),
            P("seq", "mp"),
            P("seq", "mp"),
        ),
        check_vma=False,
    )
```
